256 devices in a mesh: section: 8 (over x, core), seq: 32 (over z, y).
Axes of the slice: x: 4, y: 4, z: 8, core: 2. Of those that a mesh axis runs over, the one named last changes fastest.
Arguments:
- incoming: bfloat16 [4, 32, 16, 24, 320], P(None, 'seq'), may hold values from -6 to 6
- plan: int32 [4], replicated, may hold values from 0 to 3, each once
- waiting: bfloat16 [8, 32, 16, 24, 320], P('section', 'seq'), may hold values from -6 to 6
- spatial_weight: bfloat16 [8, 2, 9, 320, 320], P('section'), may hold values from -0.109375 to 0.109375
- temporal_weight: bfloat16 [8, 2, 3, 320, 320], P('section'), may hold values from -0.1875 to 0.1875
- attn_in: bfloat16 [8, 320, 960], P('section'), may hold values from -5 to 5
- attn_out: bfloat16 [8, 320, 320], P('section'), may hold values from -0.3125 to 0.3125
Outputs:
- outputs: bfloat16 [3, 8, 32, 16, 24, 320], P(None, 'section', 'seq')
The draws below stay inside these ranges and needn't reach their ends.
Inputs may be any that keep to these rules, and one draw needn't show every extreme that they name: `plan`: each of the 4 clip numbers appears once.
All inputs are finite; a program needn't handle non-finite values.
Results may differ from the reference program's by a relative error of at most 0.02.
Values may be sent and summed in bfloat16 or wider, within the bound.
A program may use at most 64 MiB of HBM per device.

```python
import jax
import jax.numpy as jnp
from jax import lax

C = 320
HEADS = 5
GROUPS = 32
H = 16
W = 24
TICKS = 3
CLIPS = 4
FRAMES = 32
N_SECTION = 8


def draw_attn_in(key, part):
    first_key = jax.random.fold_in(key, 0)
    base = jax.random.normal(first_key, (N_SECTION, C, 3 * C), jnp.float32) * C ** (-0.5)
    return jnp.clip(base, -5.0, 5.0).astype(jnp.bfloat16)


def shard_levels(own_key, extent, cuts, low, high):
    level, own = 1.0, jax.random.fold_in(own_key, 6)
    for dim, blocks in cuts:
        heights = jnp.exp(jax.random.uniform(jax.random.fold_in(own, dim), (blocks,), jnp.float32, low / len(cuts), high / len(cuts)))
        level = level * jnp.repeat(heights, extent[dim] // blocks).reshape([-1 if axis == dim else 1 for axis in range(len(extent))])
    return level


def noise(stream_key, extent, scale, limit, pieces=(), dtype=jnp.bfloat16):
    factor_of = shard_levels(stream_key, extent, pieces, -0.22, 0.18) if pieces else 1.0
    values = jax.random.normal(stream_key, extent, jnp.float32) * scale * factor_of
    return jnp.minimum(jnp.maximum(values, -limit), limit).astype(dtype)


def setup_inputs(seed: int = 0) -> dict:
    splits = jax.random.split(jax.random.key(seed), 8)
    incoming = noise(splits[0], (CLIPS, FRAMES, H, W, C), 1.0, 6.0, ((1, 32),))
    plan = jax.random.permutation(splits[1], CLIPS).astype(jnp.int32)
    waiting = noise(splits[2], (N_SECTION, FRAMES, H, W, C), 1.0, 6.0, ((0, 8), (1, 32)))
    spatial_weight = noise(splits[3], (N_SECTION, 2, 9, C, C), (9 * C) ** -0.5, 0.109375, ((0, 8),))
    temporal_weight = noise(splits[4], (N_SECTION, 2, 3, C, C), (3 * C) ** -0.5, 0.1875, ((0, 8),))
    attn_in = draw_attn_in(jax.random.fold_in(splits[7], 71), 0)
    attn_out = noise(splits[6], (N_SECTION, C, C), C ** -0.5, 0.3125, ((0, 8),))
    return dict(incoming=incoming, plan=plan, waiting=waiting, spatial_weight=spatial_weight, temporal_weight=temporal_weight, attn_in=attn_in, attn_out=attn_out)


EPSILON = 1e-05

def group_norm(values):
    frames, height, width, channels = values.shape
    grouped = values.astype(jnp.float32).reshape(frames, height * width, GROUPS, channels // GROUPS)
    center = lax.optimization_barrier(jnp.mean(grouped, axis=(1, 3), keepdims=True))
    spread = lax.optimization_barrier(jnp.mean(jnp.square(grouped - center), axis=(1, 3), keepdims=True))
    normed = (grouped - center) * lax.rsqrt(spread + EPSILON)
    return normed.reshape(frames, height, width, channels)

def layer_norm(values):
    floats = values.astype(jnp.float32)
    center = lax.optimization_barrier(jnp.mean(floats, axis=-1, keepdims=True))
    spread = lax.optimization_barrier(jnp.mean(jnp.square(floats - center), axis=-1, keepdims=True))
    return (floats - center) * lax.rsqrt(spread + EPSILON)

def spatial_conv(values, kernel):
    frames, height, width, channels = values.shape
    padded = jnp.pad(values, ((0, 0), (1, 1), (1, 1), (0, 0)))
    total = jnp.zeros((frames * height * width, kernel.shape[2]), jnp.float32)
    for offset in range(9):
        row_shift = offset // 3
        col_shift = offset % 3
        window = padded[:, row_shift:row_shift + height, col_shift:col_shift + width, :].reshape(-1, channels)
        total = total + jnp.dot(window, kernel[offset], preferred_element_type=jnp.float32)
    return total.reshape(frames, height, width, -1)

def temporal_conv(values, kernel):
    frames, items, channels = values.shape
    padded = jnp.pad(values, ((1, 1), (0, 0), (0, 0)))
    total = jnp.zeros((frames * items, kernel.shape[2]), jnp.float32)
    for offset in range(3):
        window = padded[offset:offset + frames].reshape(-1, channels)
        total = total + jnp.dot(window, kernel[offset], preferred_element_type=jnp.float32)
    return total.reshape(frames, items, -1)

def spatial_part(values, kernels):
    first_in = jax.nn.silu(group_norm(values)).astype(jnp.bfloat16)
    middle = spatial_conv(first_in, kernels[0]).astype(jnp.bfloat16)
    second_in = jax.nn.silu(group_norm(middle)).astype(jnp.bfloat16)
    return (values.astype(jnp.float32) + spatial_conv(second_in, kernels[1])).astype(jnp.bfloat16)

def temporal_convs(values, kernels):
    first_in = jax.nn.silu(layer_norm(values)).astype(jnp.bfloat16)
    middle = temporal_conv(first_in, kernels[0]).astype(jnp.bfloat16)
    second_in = jax.nn.silu(layer_norm(middle)).astype(jnp.bfloat16)
    return (values.astype(jnp.float32) + temporal_conv(second_in, kernels[1])).astype(jnp.bfloat16)

def attention(values, packed, outward):
    frames, items, channels = values.shape
    head_size = channels // HEADS
    normed = layer_norm(values).astype(jnp.bfloat16)
    projected = jnp.dot(normed.reshape(-1, channels), packed, preferred_element_type=jnp.float32).astype(jnp.bfloat16)
    projected = projected.reshape(frames, items, 3, HEADS, head_size)
    queries = projected[:, :, 0].astype(jnp.float32)
    keys_all = projected[:, :, 1].astype(jnp.float32)
    values_all = projected[:, :, 2].astype(jnp.float32)
    scores = jnp.einsum('fkhd,gkhd->khfg', queries, keys_all) * head_size ** (-0.5)
    weights = jax.nn.softmax(scores, axis=-1).astype(jnp.bfloat16)
    mixed = jnp.einsum('khfg,gkhd->fkhd', weights.astype(jnp.float32), values_all).astype(jnp.bfloat16)
    result = values.astype(jnp.float32).reshape(-1, channels) + jnp.dot(mixed.reshape(-1, channels), outward, preferred_element_type=jnp.float32)
    return result.reshape(frames, items, channels).astype(jnp.bfloat16)

def section_block(clip, spatial_kernels, temporal_kernels, packed, outward):
    frames, height, width, channels = clip.shape
    after_spatial = spatial_part(clip, spatial_kernels)
    flat = after_spatial.reshape(frames, height * width, channels)
    after_convs = temporal_convs(flat, temporal_kernels)
    finished = attention(after_convs, packed, outward)
    return finished.reshape(frames, height, width, channels)

def reference(incoming, plan, waiting, spatial_weight, temporal_weight, attn_in, attn_out):
    current = [waiting[section_number] for section_number in range(N_SECTION)]
    collected = []
    previous = current
    for tick_index in range(TICKS):
        if tick_index > 0:
            entering = lax.dynamic_index_in_dim(incoming, plan[tick_index - 1], 0, keepdims=False)
            current = [entering] + previous[:-1]
        previous = [section_block(current[section_number], spatial_weight[section_number], temporal_weight[section_number], attn_in[section_number], attn_out[section_number]) for section_number in range(N_SECTION)]
        collected.append(jnp.stack(previous))
    return jnp.stack(collected)
```

```python
import functools

import jax
import jax.numpy as jnp
from jax import lax
from jax.experimental import pallas as pl
from jax.experimental.pallas import tpu as pltpu
from jax.sharding import PartitionSpec as P

HEADS = 5
TICKS = 3
SEQ = 32
SECTIONS = 8
EPSILON = 1e-05
C = 320
CM = 256
CT = 64
W = 24
H = 16
CELLS = H * W
NA = 8
NB = 4
ROWS_A = SEQ * NA
ROWS_B = SEQ * NB
FAR = -1e30
MESH = pl.DeviceIdType.MESH
F32 = jnp.float32
BF16 = jnp.bfloat16


def dot(a, b):
    return jnp.dot(a, b, preferred_element_type=F32)


def silu(v):
    return v * (0.5 * jnp.tanh(0.5 * v) + 0.5)


def layer_norm(v):
    center = jnp.mean(v, axis=-1, keepdims=True)
    d = v - center
    spread = jnp.mean(d * d, axis=-1, keepdims=True)
    return d * lax.rsqrt(spread + EPSILON)


def group_norm(v, groups):
    count = 1.0 / (v.shape[0] * 10)

    def over_group(rows):
        wide = jnp.broadcast_to(rows, (8, C))
        total = jnp.dot(wide, groups, preferred_element_type=F32, precision=lax.Precision.HIGHEST)
        return total[0:1] * count

    center = over_group(jnp.sum(v, axis=0, keepdims=True))
    d = v - center
    spread = over_group(jnp.sum(d * d, axis=0, keepdims=True))
    return d * lax.rsqrt(spread + EPSILON)


def tails(a, b, c):
    zero = jnp.zeros_like(a)
    first = jnp.concatenate([a, zero], axis=1) + pltpu.roll(jnp.concatenate([b, zero], axis=1), CT, 1)
    return jnp.concatenate([first, c], axis=1)


def fill_taps(y, x_ref):
    main = y[:, :CM].astype(BF16)
    x_ref[W:, 0:CM] = main[: CELLS - W]
    x_ref[:, CM : 2 * CM] = main
    x_ref[: CELLS - W, 2 * CM : 3 * CM] = main[W:]
    tail = y[:, CM:]
    edge = jnp.zeros((W, CT), F32)
    above = jnp.concatenate([edge, tail[: CELLS - W]], axis=0)
    below = jnp.concatenate([tail[W:], edge], axis=0)
    x_ref[:, 3 * CM :] = tails(above, tail, below).astype(BF16)


def column_taps(p):
    rows = p.shape[0]
    high = rows // W

    def add(left, mid, right):
        width = left.shape[1]
        col = lax.broadcasted_iota(jnp.int32, (high, W, width), 1)
        left = pltpu.roll(left, 1, 0).reshape(high, W, width)
        right = pltpu.roll(right, rows - 1, 0).reshape(high, W, width)
        left = jnp.where(col > 0, left, 0.0).reshape(rows, width)
        right = jnp.where(col < W - 1, right, 0.0).reshape(rows, width)
        return mid + left + right

    main = add(p[:, 0:CM], p[:, CM : 2 * CM], p[:, 2 * CM : 3 * CM])
    pair = p[:, 3 * CM : 3 * CM + 2 * CT]
    mid = pltpu.roll(pair, CT, 1)[:, :CT]
    tail = add(pair[:, :CT], mid, p[:, 3 * CM + 2 * CT :])
    return jnp.concatenate([main, tail], axis=1)


def temporal_dot(act, cells, w):
    rows = act.shape[0]
    row = lax.broadcasted_iota(jnp.int32, (rows, C), 0)
    before = jnp.where(row >= cells, pltpu.roll(act, cells, 0), 0.0)
    after = jnp.where(row < rows - cells, pltpu.roll(act, rows - cells, 0), 0.0)
    lhs = jnp.concatenate(
        [
            before[:, :CM].astype(BF16),
            act[:, :CM].astype(BF16),
            after[:, :CM].astype(BF16),
            tails(before[:, CM:], act[:, CM:], after[:, CM:]).astype(BF16),
        ],
        axis=1,
    )
    return dot(lhs, w)


def temporal_part(x1, cells, tw_ref, wi_ref, wo_ref, bias_ref):
    rows = x1.shape[0]
    x1 = x1.astype(F32)
    u = temporal_dot(silu(layer_norm(x1)), cells, tw_ref[0]).astype(BF16).astype(F32)
    x2 = (x1 + temporal_dot(silu(layer_norm(u)), cells, tw_ref[1])).astype(BF16).astype(F32)
    proj = dot(layer_norm(x2).astype(BF16), wi_ref[...])
    lane = lax.broadcasted_iota(jnp.int32, (rows, 2 * CT), 1)
    low = lane < CT
    bias = bias_ref[...]
    scale = 0.125 * 1.4426950408889634

    def weights(q, k):
        s = lax.dot_general(q, k, (((1,), (1,)), ((), ())), preferred_element_type=F32) + bias
        top = jnp.max(s, axis=-1, keepdims=True)
        return jnp.exp2((s - top) * scale).astype(BF16)

    mixed = []
    for pair in range(3):
        q = proj[:, 128 * pair : 128 * pair + 128]
        k = proj[:, 384 + 128 * pair : 512 + 128 * pair].astype(BF16)
        if pair < 2:
            v = proj[:, 768 + 128 * pair : 896 + 128 * pair]
        else:
            v = pltpu.roll(q, CT, 1)
        even = dot(weights(jnp.where(low, q, 0.0).astype(BF16), k), jnp.where(low, v, 1.0).astype(BF16))
        if pair < 2:
            odd = dot(weights(jnp.where(low, 0.0, q).astype(BF16), k), jnp.where(low, 1.0, v).astype(BF16))
            total = pltpu.roll(jnp.where(low, odd, even), CT, 1)
            mixed.append((jnp.where(low, even, odd) / total).astype(BF16))
        else:
            mixed.append((even / pltpu.roll(even, CT, 1)).astype(BF16)[:, :CT])
    mixed = jnp.concatenate(mixed, axis=1)
    return (x2 + dot(mixed, wo_ref[...])).astype(BF16)


def body(
    inc_hbm, plan, wait_hbm, sw_hbm, tw_hbm, ai_hbm, ao_hbm, out_hbm,
    inc, xi, xs, sw, tw, ai, ao, wc, wi, groups, bias_a, bias_b, taps,
    sa, sb, fa, fb, ta, tb, ra, rb,
    in_sem, fs_sem, fr_sem, rs_sem, rr_sem, os_sem, or_sem,
):
    me = lax.axis_index("seq")
    section = lax.axis_index("section")
    nxt = lax.rem(section + 1, SECTIONS)
    prv = lax.rem(section + SECTIONS - 1, SECTIONS)

    loads = [
        pltpu.make_async_copy(wait_hbm, xi, in_sem.at[0]),
        pltpu.make_async_copy(sw_hbm.at[0], sw.at[0], in_sem.at[1]),
        pltpu.make_async_copy(sw_hbm.at[1], sw.at[1], in_sem.at[2]),
        pltpu.make_async_copy(ai_hbm, ai, in_sem.at[3]),
        pltpu.make_async_copy(ao_hbm, ao, in_sem.at[4]),
        pltpu.make_async_copy(inc_hbm, inc, in_sem.at[5]),
    ]
    slot = 6
    for k in range(2):
        for i in range(3):
            loads.append(pltpu.make_async_copy(
                tw_hbm.at[k, i, pl.ds(0, CM)], tw.at[k, pl.ds(CM * i, CM)], in_sem.at[slot]))
            loads.append(pltpu.make_async_copy(
                tw_hbm.at[k, i, pl.ds(CM, CT)], tw.at[k, pl.ds(3 * CM + CT * i, CT)], in_sem.at[slot + 1]))
            slot += 2
    for load in loads:
        load.start()

    barrier = pltpu.get_barrier_semaphore()

    def greet(k, carry):
        pl.semaphore_signal(barrier, 1, device_id={"section": nxt, "seq": k}, device_id_type=MESH)

        @pl.when(k != me)
        def _():
            pl.semaphore_signal(barrier, 1, device_id={"section": section, "seq": k}, device_id_type=MESH)

        return carry

    lax.fori_loop(0, SEQ, greet, 0)
    pl.semaphore_signal(barrier, 1, device_id={"section": prv, "seq": me}, device_id_type=MESH)

    row = lax.broadcasted_iota(jnp.int32, (C, C), 0)
    col = lax.broadcasted_iota(jnp.int32, (C, C), 1)
    groups[...] = jnp.where((row * 6554) // 65536 == (col * 6554) // 65536, 1.0, 0.0)
    taps[...] = jnp.zeros_like(taps)
    for ref, cells in ((bias_a, NA), (bias_b, NB)):
        r = lax.broadcasted_iota(jnp.int32, ref.shape, 0)
        c = lax.broadcasted_iota(jnp.int32, ref.shape, 1)
        ref[...] = jnp.where((r & (cells - 1)) == (c & (cells - 1)), 0.0, FAR)

    def pack_conv(k):
        for i in range(3):
            part = [sw[k, 3 * i + j] for j in range(3)]
            side = tails(*[t[:, CM:].astype(F32) for t in part]).astype(BF16)
            whole = jnp.concatenate([t[:, :CM] for t in part] + [side], axis=1)
            wc[k, CM * i : CM * i + CM] = whole[:CM]
            wc[k, 3 * CM + CT * i : 3 * CM + CT * i + CT] = whole[CM:]

    def pack_attn():
        whole = ai[...].astype(F32)
        q = whole[:, :256]
        cross = whole[:, 256:384]
        mid = whole[:, 384:640]
        v = whole[:, 640:896]
        last = jnp.concatenate([whole[:, 896:960], jnp.zeros((C, CT), F32)], axis=1)
        low = lax.broadcasted_iota(jnp.int32, (C, 128), 1) < CT
        turned = [pltpu.roll(t, CT, 1) for t in (cross, mid[:, :128], mid[:, 128:])]
        wi[:, 0:256] = q.astype(BF16)
        wi[:, 256:384] = jnp.where(low, cross, pltpu.roll(last, CT, 1)).astype(BF16)
        wi[:, 384:512] = jnp.where(low, turned[0], turned[1]).astype(BF16)
        wi[:, 512:640] = jnp.where(low, turned[1], turned[2]).astype(BF16)
        wi[:, 640:768] = jnp.where(low, turned[2], 0.0).astype(BF16)
        wi[:, 768:1024] = v.astype(BF16)

    def send_forward(t, src, dst, lane):
        def one(k, carry):
            to = lax.rem(me + k, SEQ)
            pltpu.make_async_remote_copy(
                src.at[t, to], dst.at[t, me], fs_sem.at[lane, t], fr_sem.at[lane, t],
                device_id={"section": section, "seq": to}, device_id_type=MESH).start()
            return carry

        pltpu.make_async_copy(src.at[t, me], dst.at[t, me], fr_sem.at[lane, t]).start()
        lax.fori_loop(1, SEQ, one, 0)

    def send_back(t, src, dst, lane):
        target = jnp.where(t < TICKS - 1, nxt, section)

        def one(k, carry):
            to = lax.rem(me + k, SEQ)
            pltpu.make_async_remote_copy(
                src.at[t, to], dst.at[t, me], rs_sem.at[lane, t], rr_sem.at[lane, t],
                device_id={"section": target, "seq": to}, device_id_type=MESH).start()
            return carry

        @pl.when(t < TICKS - 1)
        def _():
            one(0, 0)

        @pl.when(t == TICKS - 1)
        def _():
            pltpu.make_async_copy(src.at[t, me], dst.at[t, me], rr_sem.at[lane, t]).start()

        lax.fori_loop(1, SEQ, one, 0)

    def whole(ref, sem):
        pltpu.make_async_copy(ref, ref, sem).wait()

    loads[0].wait()

    def tick(t, carry):
        x = xi[...].astype(F32)
        fill_taps(silu(group_norm(x, groups[...])), taps)

        @pl.when(t == 0)
        def _():
            loads[1].wait()
            pack_conv(0)
            loads[2].wait()
            pack_conv(1)

        a = column_taps(dot(taps[...], wc[0])).astype(BF16).astype(F32)
        fill_taps(silu(group_norm(a, groups[...])), taps)
        got = column_taps(dot(taps[0 : 11 * W], wc[1]))
        sa[t] = (x[:ROWS_A] + got[:ROWS_A]).astype(BF16).reshape(SEQ, NA, C)

        @pl.when(t == 0)
        def _():
            pl.semaphore_wait(barrier, 2 * SEQ)

        send_forward(t, sa, fa, 0)
        got = column_taps(dot(taps[10 * W :], wc[1]))
        sb[t] = (x[ROWS_A:] + got[ROWS_A - 10 * W :]).astype(BF16).reshape(SEQ, NB, C)
        send_forward(t, sb, fb, 1)

        @pl.when(t == 0)
        def _():
            for load in loads[3:]:
                load.wait()
            pack_attn()

        whole(fa.at[t], fr_sem.at[0, t])
        done = temporal_part(fa[t].reshape(ROWS_A, C), NA, tw, wi, ao, bias_a)
        ta[t] = done.reshape(SEQ, NA, C)
        send_back(t, ta, ra, 0)
        whole(fb.at[t], fr_sem.at[1, t])
        done = temporal_part(fb[t].reshape(ROWS_B, C), NB, tw, wi, ao, bias_b)
        tb[t] = done.reshape(SEQ, NB, C)
        send_back(t, tb, rb, 1)
        whole(ra.at[t], rr_sem.at[0, t])
        whole(rb.at[t], rr_sem.at[1, t])
        xs[t, 0:ROWS_A] = ra[t].reshape(ROWS_A, C)
        xs[t, ROWS_A:] = rb[t].reshape(ROWS_B, C)

        @pl.when(t < TICKS - 1)
        def _():
            pltpu.make_async_remote_copy(
                xs.at[t], out_hbm.at[t], os_sem.at[t], or_sem.at[t],
                device_id={"section": prv, "seq": me}, device_id_type=MESH).start()
            xi[...] = jnp.where(section == 0, inc[plan[t]], xs[t])

        return carry

    lax.fori_loop(0, TICKS, tick, 0)
    last = pltpu.make_async_copy(xs.at[TICKS - 1], out_hbm.at[TICKS - 1], os_sem.at[TICKS - 1])
    last.start()
    for t in range(TICKS):
        for lane, (src, back) in enumerate(((sa, ta), (sb, tb))):
            part = src.at[t, pl.ds(0, SEQ - 1)]
            pltpu.make_async_copy(part, part, fs_sem.at[lane, t]).wait()
            part = back.at[t, pl.ds(0, SEQ - 1 if t == TICKS - 1 else SEQ)]
            pltpu.make_async_copy(part, part, rs_sem.at[lane, t]).wait()
    for t in range(TICKS - 1):
        pltpu.make_async_copy(xs.at[t], xs.at[t], os_sem.at[t]).wait()
        pltpu.make_async_copy(out_hbm.at[t], out_hbm.at[t], or_sem.at[t]).wait()
    last.wait()


def shards(incoming, plan, waiting, spatial_weight, temporal_weight, attn_in, attn_out):
    hbm = pl.BlockSpec(memory_space=pl.ANY)
    steps = (TICKS,)
    out = pl.pallas_call(
        body,
        out_shape=jax.ShapeDtypeStruct((TICKS, CELLS, C), BF16),
        in_specs=[hbm, pl.BlockSpec(memory_space=pltpu.SMEM), hbm, hbm, hbm, hbm, hbm],
        out_specs=hbm,
        scratch_shapes=[
            pltpu.VMEM((4, CELLS, C), BF16),
            pltpu.VMEM((CELLS, C), BF16),
            pltpu.VMEM(steps + (CELLS, C), BF16),
            pltpu.VMEM((2, 9, C, C), BF16),
            pltpu.VMEM((2, 3 * C, C), BF16),
            pltpu.VMEM((C, 3 * C), BF16),
            pltpu.VMEM((C, C), BF16),
            pltpu.VMEM((2, 3 * C, 3 * C), BF16),
            pltpu.VMEM((C, 1024), BF16),
            pltpu.VMEM((C, C), F32),
            pltpu.VMEM((ROWS_A, ROWS_A), F32),
            pltpu.VMEM((ROWS_B, ROWS_B), F32),
            pltpu.VMEM((CELLS, 3 * C), BF16),
        ]
        + [pltpu.VMEM(steps + (SEQ, n, C), BF16) for _ in range(4) for n in (NA, NB)]
        + [
            pltpu.SemaphoreType.DMA((18,)),
            pltpu.SemaphoreType.DMA((2, TICKS)),
            pltpu.SemaphoreType.DMA((2, TICKS)),
            pltpu.SemaphoreType.DMA((2, TICKS)),
            pltpu.SemaphoreType.DMA((2, TICKS)),
            pltpu.SemaphoreType.DMA((TICKS,)),
            pltpu.SemaphoreType.DMA((TICKS,)),
        ],
        compiler_params=pltpu.CompilerParams(
            collective_id=0, has_side_effects=True, vmem_limit_bytes=60 * 1024 * 1024),
    )(
        incoming.reshape(4, CELLS, C), plan, waiting.reshape(CELLS, C),
        spatial_weight[0], temporal_weight[0], attn_in[0], attn_out[0],
    )
    return out.reshape(TICKS, 1, 1, H, W, C)


def solution(mesh):
    return jax.shard_map(
        shards,
        mesh=mesh,
        in_specs=(
            P(None, "seq", None, None, None),
            P(),
            P("section", "seq", None, None, None),
            P("section", None, None, None, None),
            P("section", None, None, None, None),
            P("section", None, None),
            P("section", None, None),
        ),
        out_specs=P(None, "section", "seq", None, None, None),
        check_vma=False,
    )
```

```python
import jax
import jax.numpy as jnp
from jax import lax
from jax.experimental import pallas as pl
from jax.experimental.pallas import tpu as pltpu
from jax.sharding import PartitionSpec as P

TICKS = 3
SEQ = 32
NY = 4
NZ = 8
SECTIONS = 8
EPSILON = 1e-05
C = 320
CM = 256
CT = 64
W = 24
H = 16
CELLS = H * W
NA = 4
NB = 2
ROWS_A = SEQ * NA * 2
ROWS_B = SEQ * NB * 2
BLOCK = 128
PIVOT = ROWS_A
FAR = -1e30
MESH = pl.DeviceIdType.MESH
F32 = jnp.float32
BF16 = jnp.bfloat16


def hops(offset):
    dz, dy = offset
    return min(dz, NZ - dz) + min(dy, NY - dy)


OFFSETS = sorted(
    [(dz, dy) for dz in range(NZ) for dy in range(NY) if (dz, dy) != (0, 0)], key=lambda o: -hops(o)
)


def dot(a, b):
    return jnp.dot(a, b, preferred_element_type=F32)


def silu_of_half(h):
    return h * jnp.tanh(h) + h


def layer_norm(v, factor):
    center = jnp.mean(v, axis=-1, keepdims=True)
    d = v - center
    spread = jnp.mean(d * d, axis=-1, keepdims=True)
    return d * (factor * lax.rsqrt(spread + EPSILON))


def over_groups(rows, groups):
    high = rows.astype(BF16).astype(F32)
    rest = rows - high
    mid = rest.astype(BF16).astype(F32)
    low = rest - mid
    parts = jnp.concatenate([high, mid, low, jnp.zeros_like(low)], axis=0).astype(BF16)
    got = dot(parts, groups)
    return got[0:2] + got[2:4] + got[4:6]


def find_pivot(v, groups):
    total = jnp.sum(v, axis=0, keepdims=True)
    return over_groups(jnp.concatenate([total, total], axis=0), groups)[0:1] * (1.0 / (v.shape[0] * 10))


def group_norm_half(v, pivot, groups):
    count = 1.0 / (CELLS * 10)
    d = v - pivot
    sums = jnp.concatenate([jnp.sum(d, axis=0, keepdims=True), jnp.sum(d * d, axis=0, keepdims=True)], axis=0)
    means = over_groups(sums, groups) * count
    shift = means[0:1]
    spread = jnp.maximum(means[1:2] - shift * shift, 0.0)
    scale = 0.5 * lax.rsqrt(spread + EPSILON)
    return d * scale - shift * scale


def side_by_side(a, b):
    zero = jnp.zeros_like(a)
    return jnp.concatenate([a, zero], axis=1) + pltpu.roll(jnp.concatenate([b, zero], axis=1), CT, 1)


def tails(a, b, c):
    return jnp.concatenate([side_by_side(a, b), c], axis=1)


def fill_taps(y, x_ref):
    main = y[:, :CM].astype(BF16)
    x_ref[W:, 0:CM] = main[: CELLS - W]
    x_ref[:, CM : 2 * CM] = main
    x_ref[: CELLS - W, 2 * CM : 3 * CM] = main[W:]
    tail = y[:, CM:]
    edge = jnp.zeros((W, CT), F32)
    above = jnp.concatenate([edge, tail[: CELLS - W]], axis=0)
    below = jnp.concatenate([tail[W:], edge], axis=0)
    x_ref[:, 3 * CM :] = tails(above, tail, below).astype(BF16)


def column_taps(p):
    rows = p.shape[0]
    high = rows // W

    def add(left, mid, right):
        width = left.shape[1]
        col = lax.broadcasted_iota(jnp.int32, (high, W, width), 1)
        left = pltpu.roll(left, 1, 0).reshape(high, W, width)
        right = pltpu.roll(right, rows - 1, 0).reshape(high, W, width)
        left = jnp.where(col > 0, left, 0.0).reshape(rows, width)
        right = jnp.where(col < W - 1, right, 0.0).reshape(rows, width)
        return mid + left + right

    main = add(p[:, 0:CM], p[:, CM : 2 * CM], p[:, 2 * CM : 3 * CM])
    pair = p[:, 3 * CM : 3 * CM + 2 * CT]
    mid = pltpu.roll(pair, CT, 1)[:, :CT]
    tail = add(pair[:, :CT], mid, p[:, 3 * CM + 2 * CT :])
    return jnp.concatenate([main, tail], axis=1)


def pack(v):
    half = v.shape[0] // 2
    low, high = v[:half], v[half:]
    return jnp.concatenate(
        [low[:, :CM].astype(BF16), high[:, :CM].astype(BF16), side_by_side(low[:, CM:], high[:, CM:]).astype(BF16)],
        axis=1,
    )


def unpack(p):
    p = p.astype(F32)
    side = p[:, 2 * CM :]
    low = jnp.concatenate([p[:, :CM], side[:, :CT]], axis=1)
    high = jnp.concatenate([p[:, CM : 2 * CM], pltpu.roll(side, CT, 1)[:, :CT]], axis=1)
    return jnp.concatenate([low, high], axis=0)


def temporal_dot(act, cells, w):
    rows = act.shape[0]
    half = rows // 2
    row = lax.broadcasted_iota(jnp.int32, (rows, C), 0) & (half - 1)
    before = jnp.where(row >= cells, pltpu.roll(act, cells, 0), 0.0)
    after = jnp.where(row < half - cells, pltpu.roll(act, rows - cells, 0), 0.0)
    lhs = jnp.concatenate(
        [
            before[:, :CM].astype(BF16),
            act[:, :CM].astype(BF16),
            after[:, :CM].astype(BF16),
            tails(before[:, CM:], act[:, CM:], after[:, CM:]).astype(BF16),
        ],
        axis=1,
    )
    return dot(lhs, w)


def attention(proj, bias):
    low = lax.broadcasted_iota(jnp.int32, (BLOCK, 2 * CT), 1) < CT
    scale = 0.125 * 1.4426950408889634
    scores, held = [], []
    for pair in range(3):
        q = proj[:, 128 * pair : 128 * pair + 128]
        k = proj[:, 384 + 128 * pair : 512 + 128 * pair].astype(BF16)
        v = proj[:, 768 + 128 * pair : 896 + 128 * pair] if pair < 2 else pltpu.roll(q, CT, 1)
        for side in range(2 if pair < 2 else 1):
            own = low if side == 0 else jnp.logical_not(low)
            one = jnp.where(own, q, 0.0).astype(BF16)
            scores.append(lax.dot_general(one, k, (((1,), (1,)), ((), ())), preferred_element_type=F32) + bias)
            held.append(jnp.where(own, v, 1.0).astype(BF16))
    tops = [jnp.max(s, axis=-1, keepdims=True) for s in scores]
    weights = [jnp.exp2((s - top) * scale).astype(BF16) for s, top in zip(scores, tops)]
    got = [dot(w, v) for w, v in zip(weights, held)]
    mixed = []
    for pair in range(2):
        even, odd = got[2 * pair], got[2 * pair + 1]
        total = pltpu.roll(jnp.where(low, odd, even), CT, 1)
        mixed.append((jnp.where(low, even, odd) / total).astype(BF16))
    mixed.append((got[4] / pltpu.roll(got[4], CT, 1)).astype(BF16)[:, :CT])
    return jnp.concatenate(mixed, axis=1)


def temporal_part(x1, cells, tw_ref, wi_ref, wo_ref, bias_ref):
    u = temporal_dot(silu_of_half(layer_norm(x1, 0.5)), cells, tw_ref[0]).astype(BF16).astype(F32)
    x2 = (x1 + temporal_dot(silu_of_half(layer_norm(u, 0.5)), cells, tw_ref[1])).astype(BF16).astype(F32)
    proj = dot(layer_norm(x2, 1.0).astype(BF16), wi_ref[...])
    bias = bias_ref[...]
    mixed = [attention(proj[at : at + BLOCK], bias) for at in range(0, x1.shape[0], BLOCK)]
    mixed = mixed[0] if len(mixed) == 1 else jnp.concatenate(mixed, axis=0)
    return x2 + dot(mixed, wo_ref[...])


def body(
    inc_hbm, plan, wait_hbm, sw_hbm, tw_hbm, ai_hbm, ao_hbm, out0, out1, out2,
    inc, xi, xs, sw, tw, ai, ao, wc, wi, groups, pivot, bias_a, bias_b, taps,
    sa, sb, fa, fb, ta, tb, ra, rb,
    in_sem, fs_sem, fr_sem, rs_sem, rr_sem, os_sem, or_sem, ready,
):
    me = lax.axis_index("seq")
    section = lax.axis_index("section")
    nxt = lax.rem(section + 1, SECTIONS)
    prv = lax.rem(section + SECTIONS - 1, SECTIONS)
    my_z = me // NY
    my_y = lax.rem(me, NY)

    def peer(offset):
        dz, dy = offset
        return lax.rem(my_z + dz, NZ) * NY + lax.rem(my_y + dy, NY)

    barrier = pltpu.get_barrier_semaphore()
    for offset in OFFSETS:
        pl.semaphore_signal(barrier, 1, device_id={"section": section, "seq": peer(offset)}, device_id_type=MESH)
    for other in (nxt, prv):
        pl.semaphore_signal(barrier, 1, device_id={"section": other, "seq": me}, device_id_type=MESH)

    loads = [
        pltpu.make_async_copy(wait_hbm, xi, in_sem.at[0]),
        pltpu.make_async_copy(sw_hbm.at[0], sw.at[0], in_sem.at[1]),
        pltpu.make_async_copy(sw_hbm.at[1], sw.at[1], in_sem.at[2]),
        pltpu.make_async_copy(ai_hbm, ai, in_sem.at[3]),
        pltpu.make_async_copy(ao_hbm, ao, in_sem.at[4]),
        pltpu.make_async_copy(inc_hbm, inc, in_sem.at[5]),
    ]
    slot = 6
    for k in range(2):
        for i in range(3):
            loads.append(pltpu.make_async_copy(
                tw_hbm.at[k, i, pl.ds(0, CM)], tw.at[k, pl.ds(CM * i, CM)], in_sem.at[slot]))
            loads.append(pltpu.make_async_copy(
                tw_hbm.at[k, i, pl.ds(CM, CT)], tw.at[k, pl.ds(3 * CM + CT * i, CT)], in_sem.at[slot + 1]))
            slot += 2
    for load in loads:
        load.start()

    row = lax.broadcasted_iota(jnp.int32, (C, C), 0)
    col = lax.broadcasted_iota(jnp.int32, (C, C), 1)
    groups[...] = jnp.where((row * 6554) // 65536 == (col * 6554) // 65536, 1.0, 0.0).astype(BF16)
    taps[0:W, 0:CM] = jnp.zeros((W, CM), BF16)
    taps[CELLS - W :, 2 * CM : 3 * CM] = jnp.zeros((W, CM), BF16)

    def make_bias():
        r = lax.broadcasted_iota(jnp.int32, (BLOCK, BLOCK), 0)
        c = lax.broadcasted_iota(jnp.int32, (BLOCK, BLOCK), 1)
        bias_a[...] = jnp.where((r & (NA - 1)) == (c & (NA - 1)), 0.0, FAR)
        half = SEQ * NB
        same = ((r & (NB - 1)) == (c & (NB - 1))) & ((r & half) == (c & half))
        bias_b[...] = jnp.where(same, 0.0, FAR)

    def pack_conv(k):
        for i in range(3):
            part = [sw[k, 3 * i + j] for j in range(3)]
            side = tails(*[t[:, CM:].astype(F32) for t in part]).astype(BF16)
            whole = jnp.concatenate([t[:, :CM] for t in part] + [side], axis=1)
            wc[k, CM * i : CM * i + CM] = whole[:CM]
            wc[k, 3 * CM + CT * i : 3 * CM + CT * i + CT] = whole[CM:]

    def pack_attn():
        whole = ai[...].astype(F32)
        cross = whole[:, 256:384]
        mid = whole[:, 384:640]
        last = jnp.concatenate([whole[:, 896:960], jnp.zeros((C, CT), F32)], axis=1)
        low = lax.broadcasted_iota(jnp.int32, (C, 128), 1) < CT
        turned = [pltpu.roll(t, CT, 1) for t in (cross, mid[:, :128], mid[:, 128:])]
        wi[:, 0:256] = ai[:, :256]
        wi[:, 256:384] = jnp.where(low, cross, pltpu.roll(last, CT, 1)).astype(BF16)
        wi[:, 384:512] = jnp.where(low, turned[0], turned[1]).astype(BF16)
        wi[:, 512:640] = jnp.where(low, turned[1], turned[2]).astype(BF16)
        wi[:, 640:768] = jnp.where(low, turned[2], 0.0).astype(BF16)
        wi[:, 768:1024] = ai[:, 640:896]

    def send_all(t, src, dst, to_section, send_sem, recv_sem):
        for offset in OFFSETS:
            to = peer(offset)
            pltpu.make_async_remote_copy(
                src.at[t, to], dst.at[t, me], send_sem, recv_sem,
                device_id={"section": to_section, "seq": to}, device_id_type=MESH).start()

    def send_forward(t, src, dst, lane):
        send_all(t, src, dst, section, fs_sem.at[lane, t], fr_sem.at[lane, t])
        pltpu.make_async_copy(src.at[t, me], dst.at[t, me], fr_sem.at[lane, t]).start()

    def send_back(t, src, dst, lane):
        target = jnp.where(t < TICKS - 1, nxt, section)
        send_all(t, src, dst, target, rs_sem.at[lane, t], rr_sem.at[lane, t])

        @pl.when(t < TICKS - 1)
        def _():
            pltpu.make_async_remote_copy(
                src.at[t, me], dst.at[t, me], rs_sem.at[lane, t], rr_sem.at[lane, t],
                device_id={"section": target, "seq": me}, device_id_type=MESH).start()

        @pl.when(t == TICKS - 1)
        def _():
            pltpu.make_async_copy(src.at[t, me], dst.at[t, me], rr_sem.at[lane, t]).start()

    def whole(ref, sem):
        pltpu.make_async_copy(ref, ref, sem).wait()

    loads[0].wait()
    pivot[...] = find_pivot(xi[:PIVOT].astype(F32), groups[...])

    def tick(t, carry):
        x = xi[...].astype(F32)
        fill_taps(silu_of_half(group_norm_half(x, pivot[...], groups[...])), taps)

        @pl.when(t == 0)
        def _():
            loads[1].wait()
            pack_conv(0)
            loads[2].wait()
            pack_conv(1)

        top = 11 * W
        a = column_taps(dot(taps[...], wc[0])).astype(BF16).astype(F32)
        fill_taps(silu_of_half(group_norm_half(a, find_pivot(a[:PIVOT], groups[...]), groups[...])), taps)
        got = column_taps(dot(taps[0:top], wc[1]))
        sa[t] = pack(x[:ROWS_A] + got[:ROWS_A]).reshape(SEQ, NA, 2 * C)

        @pl.when(t == 0)
        def _():
            pl.semaphore_wait(barrier, SEQ + 1)

        send_forward(t, sa, fa, 0)
        got = column_taps(dot(taps[top - W :], wc[1]))
        sb[t] = pack(x[ROWS_A:] + got[ROWS_A - top + W :]).reshape(SEQ, NB, 2 * C)
        send_forward(t, sb, fb, 1)

        @pl.when(t == 0)
        def _():
            make_bias()
            for load in loads[3:]:
                load.wait()
            pack_attn()

        whole(fa.at[t], fr_sem.at[0, t])

        @pl.when(t == 0)
        def _():
            pl.semaphore_signal(ready, 1, device_id={"section": prv, "seq": me}, device_id_type=MESH)

        done = temporal_part(unpack(fa[t].reshape(SEQ * NA, 2 * C)), NA, tw, wi, ao, bias_a)
        ta[t] = pack(done).reshape(SEQ, NA, 2 * C)

        @pl.when(t == 0)
        def _():
            pl.semaphore_wait(ready, 1)

        send_back(t, ta, ra, 0)
        whole(fb.at[t], fr_sem.at[1, t])
        done = temporal_part(unpack(fb[t].reshape(SEQ * NB, 2 * C)), NB, tw, wi, ao, bias_b)
        tb[t] = pack(done).reshape(SEQ, NB, 2 * C)
        send_back(t, tb, rb, 1)
        whole(ra.at[t], rr_sem.at[0, t])
        came = unpack(ra[t].reshape(SEQ * NA, 2 * C)).astype(BF16)
        xs[t, 0:ROWS_A] = came
        came = jnp.where(section == 0, inc[plan[t], 0:ROWS_A], came)
        xi[0:ROWS_A] = came
        pivot[...] = find_pivot(came.astype(F32), groups[...])
        whole(rb.at[t], rr_sem.at[1, t])
        came = unpack(rb[t].reshape(SEQ * NB, 2 * C)).astype(BF16)
        xs[t, ROWS_A:] = came

        for early, out_ref in enumerate((out0, out1)):
            @pl.when(t == early)
            def _(early=early, out_ref=out_ref):
                pltpu.make_async_remote_copy(
                    xs.at[early], out_ref, os_sem.at[early], or_sem.at[early],
                    device_id={"section": prv, "seq": me}, device_id_type=MESH).start()

        @pl.when(t < TICKS - 1)
        def _():
            xi[ROWS_A:] = jnp.where(section == 0, inc[plan[t], ROWS_A:], xs[t, ROWS_A:])

        return carry

    lax.fori_loop(0, TICKS, tick, 0)
    last = pltpu.make_async_copy(xs.at[TICKS - 1], out2, os_sem.at[TICKS - 1])
    last.start()
    for t in range(TICKS):
        for lane, (src, back) in enumerate(((sa, ta), (sb, tb))):
            part = src.at[t, pl.ds(0, SEQ - 1)]
            pltpu.make_async_copy(part, part, fs_sem.at[lane, t]).wait()
            part = back.at[t, pl.ds(0, SEQ - 1 if t == TICKS - 1 else SEQ)]
            pltpu.make_async_copy(part, part, rs_sem.at[lane, t]).wait()
    for t, out_ref in enumerate((out0, out1)):
        pltpu.make_async_copy(xs.at[t], xs.at[t], os_sem.at[t]).wait()
        pltpu.make_async_copy(out_ref, out_ref, or_sem.at[t]).wait()
    last.wait()


def shards(incoming, plan, waiting, spatial_weight, temporal_weight, attn_in, attn_out):
    hbm = pl.BlockSpec(memory_space=pl.ANY)
    steps = (TICKS,)
    out = pl.pallas_call(
        body,
        out_shape=[jax.ShapeDtypeStruct((CELLS, C), BF16)] * TICKS,
        in_specs=[hbm, pl.BlockSpec(memory_space=pltpu.SMEM), hbm, hbm, hbm, hbm, hbm],
        out_specs=[hbm] * TICKS,
        scratch_shapes=[
            pltpu.VMEM((4, CELLS, C), BF16),
            pltpu.VMEM((CELLS, C), BF16),
            pltpu.VMEM(steps + (CELLS, C), BF16),
            pltpu.VMEM((2, 9, C, C), BF16),
            pltpu.VMEM((2, 3 * C, C), BF16),
            pltpu.VMEM((C, 3 * C), BF16),
            pltpu.VMEM((C, C), BF16),
            pltpu.VMEM((2, 3 * C, 3 * C), BF16),
            pltpu.VMEM((C, 1024), BF16),
            pltpu.VMEM((C, C), BF16),
            pltpu.VMEM((1, C), F32),
            pltpu.VMEM((BLOCK, BLOCK), F32),
            pltpu.VMEM((BLOCK, BLOCK), F32),
            pltpu.VMEM((CELLS, 3 * C), BF16),
        ]
        + [pltpu.VMEM(steps + (SEQ, n, 2 * C), BF16) for _ in range(4) for n in (NA, NB)]
        + [
            pltpu.SemaphoreType.DMA((18,)),
            pltpu.SemaphoreType.DMA((2, TICKS)),
            pltpu.SemaphoreType.DMA((2, TICKS)),
            pltpu.SemaphoreType.DMA((2, TICKS)),
            pltpu.SemaphoreType.DMA((2, TICKS)),
            pltpu.SemaphoreType.DMA((TICKS,)),
            pltpu.SemaphoreType.DMA((TICKS,)),
            pltpu.SemaphoreType.REGULAR,
        ],
        compiler_params=pltpu.CompilerParams(
            collective_id=0, has_side_effects=True, vmem_limit_bytes=60 * 1024 * 1024),
    )(
        incoming.reshape(4, CELLS, C), plan, waiting.reshape(CELLS, C),
        spatial_weight[0], temporal_weight[0], attn_in[0], attn_out[0],
    )
    return jnp.stack([one.reshape(1, 1, H, W, C) for one in out])


def solution(mesh):
    return jax.shard_map(
        shards,
        mesh=mesh,
        in_specs=(
            P(None, "seq", None, None, None),
            P(),
            P("section", "seq", None, None, None),
            P("section", None, None, None, None),
            P("section", None, None, None, None),
            P("section", None, None),
            P("section", None, None),
        ),
        out_specs=P(None, "section", "seq", None, None, None),
        check_vma=False,
    )
```

```python
import jax
import jax.numpy as jnp
from jax import lax
from jax.experimental import pallas as pl
from jax.experimental.pallas import tpu as pltpu
from jax.sharding import PartitionSpec as P

TICKS = 3
SEQ = 32
NY = 4
NZ = 8
SECTIONS = 8
EPSILON = 1e-05
C = 320
CM = 256
CT = 64
CP = 384
LANES = 128
DEEP = 1024
W = 24
H = 16
CELLS = H * W
NA = 4
NB = 2
ROWS_A = SEQ * NA * 2
ROWS_B = SEQ * NB * 2
BLOCK = 128
PIVOT = ROWS_A
FAR = -1e30
MESH = pl.DeviceIdType.MESH
F32 = jnp.float32
BF16 = jnp.bfloat16


def hops(offset):
    dz, dy = offset
    return min(dz, NZ - dz) + min(dy, NY - dy)


OFFSETS = sorted(
    [(dz, dy) for dz in range(NZ) for dy in range(NY) if (dz, dy) != (0, 0)], key=lambda o: -hops(o)
)


def dot(a, b):
    return jnp.dot(a, b, preferred_element_type=F32)


def in_low(rows):
    return lax.broadcasted_iota(jnp.int32, (rows, LANES), 1) < CT


def turn(v):
    return pltpu.roll(v, CT, 1)


def widen(v):
    return jnp.concatenate([v, jnp.zeros((v.shape[0], CP - C), v.dtype)], axis=1)


def silu_of_half(h):
    return h * jnp.tanh(h) + h


def layer_norm(v, factor):
    center = jnp.sum(v, axis=-1, keepdims=True) * (1.0 / C)
    side = jnp.where(in_low(v.shape[0]), v[:, CM:] - center, 0.0)
    d = jnp.concatenate([v[:, :CM] - center, side], axis=1)
    spread = jnp.sum(d * d, axis=-1, keepdims=True) * (1.0 / C)
    return d * (factor * lax.rsqrt(spread + EPSILON))


def over_groups(rows, groups):
    high = rows.astype(BF16).astype(F32)
    rest = rows - high
    mid = rest.astype(BF16).astype(F32)
    low = rest - mid
    parts = jnp.concatenate([high, mid, low, jnp.zeros_like(low)], axis=0).astype(BF16)
    got = dot(parts, groups)
    return got[0:2] + got[2:4] + got[4:6]


def find_pivot(v, groups):
    total = jnp.sum(v, axis=0, keepdims=True)
    return over_groups(jnp.concatenate([total, total], axis=0), groups)[0:1] * (1.0 / (v.shape[0] * 10))


def group_norm_half(v, pivot, groups):
    count = 1.0 / (CELLS * 10)
    d = v - pivot
    sums = jnp.concatenate([jnp.sum(d, axis=0, keepdims=True), jnp.sum(d * d, axis=0, keepdims=True)], axis=0)
    means = over_groups(sums, groups) * count
    shift = means[0:1]
    spread = jnp.maximum(means[1:2] - shift * shift, 0.0)
    scale = 0.5 * lax.rsqrt(spread + EPSILON)
    return d * scale - shift * scale


def fill_taps(y, x_ref):
    main = y[:, :CM].astype(BF16)
    x_ref[W:, 0:CM] = main[: CELLS - W]
    x_ref[:, CM : 2 * CM] = main
    x_ref[: CELLS - W, 2 * CM : 3 * CM] = main[W:]
    tail = y[:, CM:]
    edge = jnp.zeros((W, LANES), F32)
    above = jnp.concatenate([edge, tail[: CELLS - W]], axis=0)
    below = jnp.concatenate([tail[W:], edge], axis=0)
    x_ref[:, 3 * CM : 3 * CM + LANES] = (above + turn(tail)).astype(BF16)
    x_ref[:, 3 * CM + LANES :] = below.astype(BF16)


def column_taps(p):
    rows = p.shape[0]
    high = rows // W

    def add(left, mid, right):
        width = left.shape[1]
        col = lax.broadcasted_iota(jnp.int32, (high, W, width), 1)
        left = pltpu.roll(left, 1, 0).reshape(high, W, width)
        right = pltpu.roll(right, rows - 1, 0).reshape(high, W, width)
        left = jnp.where(col > 0, left, 0.0).reshape(rows, width)
        right = jnp.where(col < W - 1, right, 0.0).reshape(rows, width)
        return mid + left + right

    main = add(p[:, 0:CM], p[:, CM : 2 * CM], p[:, 2 * CM : 3 * CM])
    pair = p[:, 3 * CM : 3 * CM + LANES]
    tail = jnp.where(in_low(rows), add(pair, turn(pair), p[:, 3 * CM + LANES :]), 0.0)
    return jnp.concatenate([main, tail], axis=1)


def pack(v):
    half = v.shape[0] // 2
    low, high = v[:half], v[half:]
    return jnp.concatenate([low[:, :CM], high[:, :CM], low[:, CM:] + turn(high[:, CM:])], axis=1).astype(BF16)


def unpack(p):
    p = p.astype(F32)
    side = p[:, 2 * CM :]
    mask = in_low(p.shape[0])
    low = jnp.concatenate([p[:, :CM], jnp.where(mask, side, 0.0)], axis=1)
    high = jnp.concatenate([p[:, CM : 2 * CM], jnp.where(mask, turn(side), 0.0)], axis=1)
    return jnp.concatenate([low, high], axis=0)


def temporal_dot(act, cells, w):
    rows = act.shape[0]
    half = rows // 2
    row = lax.broadcasted_iota(jnp.int32, act.shape, 0) & (half - 1)
    before = jnp.where(row >= cells, pltpu.roll(act, cells, 0), 0.0)
    after = jnp.where(row < half - cells, pltpu.roll(act, rows - cells, 0), 0.0)
    lhs = jnp.concatenate(
        [before[:, :CM], act[:, :CM], after[:, :CM], before[:, CM:] + turn(act[:, CM:]), after[:, CM:]], axis=1
    )
    return dot(lhs.astype(BF16), w)


def attention(proj, bias):
    low = in_low(BLOCK)
    scale = 0.125 * 1.4426950408889634
    scores, held = [], []
    for pair in range(3):
        q = proj[:, 128 * pair : 128 * pair + 128]
        k = proj[:, 384 + 128 * pair : 512 + 128 * pair].astype(BF16)
        v = (proj[:, 768 + 128 * pair : 896 + 128 * pair] if pair < 2 else turn(q)).T.astype(BF16)
        for side in range(2 if pair < 2 else 1):
            own = low if side == 0 else jnp.logical_not(low)
            one = jnp.where(own, q, 0.0).astype(BF16)
            scores.append(lax.dot_general(k, one, (((1,), (1,)), ((), ())), preferred_element_type=F32) + bias)
            held.append(v[CT * side : CT * side + CT])
    tops = [jnp.max(s, axis=0, keepdims=True) for s in scores]
    weights = [jnp.exp2((s - top) * scale) for s, top in zip(scores, tops)]
    totals = [jnp.sum(w, axis=0, keepdims=True) for w in weights]
    mixed = [dot(v, w.astype(BF16)) * (1.0 / total) for v, w, total in zip(held, weights, totals)]
    return jnp.concatenate(mixed + [jnp.zeros((CT, BLOCK), F32)], axis=0).T.astype(BF16)


def temporal_part(x1, cells, tw_ref, wi_ref, wo_ref, bias_ref):
    u = temporal_dot(silu_of_half(layer_norm(x1, 0.5)), cells, tw_ref[0]).astype(BF16).astype(F32)
    x2 = (x1 + temporal_dot(silu_of_half(layer_norm(u, 0.5)), cells, tw_ref[1])).astype(BF16).astype(F32)
    proj = dot(layer_norm(x2, 1.0).astype(BF16), wi_ref[...])
    bias = bias_ref[...]
    mixed = [attention(proj[at : at + BLOCK], bias) for at in range(0, x1.shape[0], BLOCK)]
    mixed = mixed[0] if len(mixed) == 1 else jnp.concatenate(mixed, axis=0)
    return x2 + dot(mixed, wo_ref[...])


def body(
    inc_hbm, plan, wait_hbm, sw_hbm, tw_hbm, ai_hbm, ao_hbm, out_ref,
    inc, xi, xs, sw, tws, ai, ao, wc, tw, wi, wo, groups, pivot, bias_a, bias_b, taps,
    sa, sb, fa, fb, ta, tb, ra, rb,
    in_sem, fs_sem, fr_sem, rs_sem, rr_sem, os_sem, or_sem, ready,
):
    me = lax.axis_index("seq")
    section = lax.axis_index("section")
    nxt = lax.rem(section + 1, SECTIONS)
    prv = lax.rem(section + SECTIONS - 1, SECTIONS)
    my_z = me // NY
    my_y = lax.rem(me, NY)

    def peer(offset):
        dz, dy = offset
        return lax.rem(my_z + dz, NZ) * NY + lax.rem(my_y + dy, NY)

    barrier = pltpu.get_barrier_semaphore()
    for offset in OFFSETS:
        pl.semaphore_signal(barrier, 1, device_id={"section": section, "seq": peer(offset)}, device_id_type=MESH)
    for other in (nxt, prv):
        pl.semaphore_signal(barrier, 1, device_id={"section": other, "seq": me}, device_id_type=MESH)

    loads = [
        pltpu.make_async_copy(wait_hbm, xi, in_sem.at[0]),
        pltpu.make_async_copy(sw_hbm.at[0], sw.at[0], in_sem.at[1]),
        pltpu.make_async_copy(sw_hbm.at[1], sw.at[1], in_sem.at[2]),
        pltpu.make_async_copy(ai_hbm, ai, in_sem.at[3]),
        pltpu.make_async_copy(ao_hbm, ao, in_sem.at[4]),
        pltpu.make_async_copy(inc_hbm, inc, in_sem.at[5]),
    ]
    loads.append(pltpu.make_async_copy(tw_hbm, tws, in_sem.at[6]))
    for load in loads:
        load.start()

    row = lax.broadcasted_iota(jnp.int32, (CP, CP), 0)
    col = lax.broadcasted_iota(jnp.int32, (CP, CP), 1)
    groups[...] = jnp.where(((row * 6554) // 65536 == (col * 6554) // 65536) & (row < C), 1.0, 0.0).astype(BF16)
    taps[0:W, 0:CM] = jnp.zeros((W, CM), BF16)
    taps[CELLS - W :, 2 * CM : 3 * CM] = jnp.zeros((W, CM), BF16)

    def make_bias():
        r = lax.broadcasted_iota(jnp.int32, (BLOCK, BLOCK), 0)
        c = lax.broadcasted_iota(jnp.int32, (BLOCK, BLOCK), 1)
        bias_a[...] = jnp.where((r & (NA - 1)) == (c & (NA - 1)), 0.0, FAR)
        half = SEQ * NB
        same = ((r & (NB - 1)) == (c & (NB - 1))) & ((r & half) == (c & half))
        bias_b[...] = jnp.where(same, 0.0, FAR)

    def pack_conv(k):
        for i in range(3):
            part = [widen(sw[k, 3 * i + j]) for j in range(3)]
            side = [t[:, CM:].astype(F32) for t in part]
            whole = jnp.concatenate(
                [t[:, :CM] for t in part] + [(side[0] + turn(side[1])).astype(BF16), part[2][:, CM:]], axis=1)
            wc[k, CM * i : CM * i + CM] = whole[:CM]
            wc[k, 3 * CM + CT * i : 3 * CM + CT * i + CT] = whole[CM:]
        wc[k, 3 * C :] = jnp.zeros((DEEP - 3 * C, DEEP), BF16)

    def pack_temporal():
        for k in range(2):
            for i in range(3):
                part = widen(tws[k, i])
                tw[k, CM * i : CM * i + CM] = part[:CM]
                tw[k, 3 * CM + CT * i : 3 * CM + CT * i + CT] = part[CM:]
            tw[k, 3 * C :] = jnp.zeros((DEEP - 3 * C, CP), BF16)

    def pack_attn():
        whole = ai[...].astype(F32)
        cross = whole[:, 256:384]
        mid = whole[:, 384:640]
        last = jnp.concatenate([whole[:, 896:960], jnp.zeros((C, CT), F32)], axis=1)
        low = in_low(C)
        turned = [turn(t) for t in (cross, mid[:, :128], mid[:, 128:])]
        wi[:C, 0:256] = ai[:, :256]
        wi[:C, 256:384] = jnp.where(low, cross, turn(last)).astype(BF16)
        wi[:C, 384:512] = jnp.where(low, turned[0], turned[1]).astype(BF16)
        wi[:C, 512:640] = jnp.where(low, turned[1], turned[2]).astype(BF16)
        wi[:C, 640:768] = jnp.where(low, turned[2], 0.0).astype(BF16)
        wi[:C, 768:1024] = ai[:, 640:896]
        wi[C:] = jnp.zeros((CP - C, DEEP), BF16)
        wo[:C] = widen(ao[...])
        wo[C:] = jnp.zeros((CP - C, CP), BF16)

    def send_all(t, src, dst, to_section, send_sem, recv_sem):
        for offset in OFFSETS:
            to = peer(offset)
            pltpu.make_async_remote_copy(
                src.at[t, to], dst.at[t, me], send_sem, recv_sem,
                device_id={"section": to_section, "seq": to}, device_id_type=MESH).start()

    def send_forward(t, src, dst, lane):
        send_all(t, src, dst, section, fs_sem.at[lane, t], fr_sem.at[lane, t])
        pltpu.make_async_copy(src.at[t, me], dst.at[t, me], fr_sem.at[lane, t]).start()

    def send_back(t, src, dst, lane):
        target = jnp.where(t < TICKS - 1, nxt, section)
        send_all(t, src, dst, target, rs_sem.at[lane, t], rr_sem.at[lane, t])

        @pl.when(t < TICKS - 1)
        def _():
            pltpu.make_async_remote_copy(
                src.at[t, me], dst.at[t, me], rs_sem.at[lane, t], rr_sem.at[lane, t],
                device_id={"section": target, "seq": me}, device_id_type=MESH).start()

        @pl.when(t == TICKS - 1)
        def _():
            pltpu.make_async_copy(src.at[t, me], dst.at[t, me], rr_sem.at[lane, t]).start()

    def whole(ref, sem):
        pltpu.make_async_copy(ref, ref, sem).wait()

    loads[0].wait()
    pivot[...] = find_pivot(widen(xi[ROWS_A:].astype(F32)), groups[...])

    def tick(t, carry):
        x = widen(xi[...].astype(F32))
        fill_taps(silu_of_half(group_norm_half(x, pivot[...], groups[...])), taps)

        @pl.when(t == 0)
        def _():
            loads[1].wait()
            pack_conv(0)
            loads[2].wait()
            pack_conv(1)

        top = 11 * W
        a = column_taps(dot(taps[...], wc[0])).astype(BF16).astype(F32)
        fill_taps(silu_of_half(group_norm_half(a, find_pivot(a[:PIVOT], groups[...]), groups[...])), taps)
        got = column_taps(dot(taps[top - W :], wc[1]))
        sb[t] = pack(x[ROWS_A:] + got[ROWS_A - top + W :]).reshape(SEQ, NB, 2 * C)

        @pl.when(t == 0)
        def _():
            pl.semaphore_wait(barrier, SEQ + 1)

        send_forward(t, sb, fb, 1)
        got = column_taps(dot(taps[0:top], wc[1]))
        sa[t] = pack(x[:ROWS_A] + got[:ROWS_A]).reshape(SEQ, NA, 2 * C)
        send_forward(t, sa, fa, 0)

        @pl.when(t == 0)
        def _():
            make_bias()
            for load in loads[3:]:
                load.wait()
            pack_temporal()
            pack_attn()

        whole(fb.at[t], fr_sem.at[1, t])

        @pl.when(t == 0)
        def _():
            pl.semaphore_signal(ready, 1, device_id={"section": prv, "seq": me}, device_id_type=MESH)

        done = temporal_part(unpack(fb[t].reshape(SEQ * NB, 2 * C)), NB, tw, wi, wo, bias_b)
        tb[t] = pack(done).reshape(SEQ, NB, 2 * C)

        @pl.when(t == 0)
        def _():
            pl.semaphore_wait(ready, 1)

        send_back(t, tb, rb, 1)
        whole(fa.at[t], fr_sem.at[0, t])
        done = temporal_part(unpack(fa[t].reshape(SEQ * NA, 2 * C)), NA, tw, wi, wo, bias_a)
        ta[t] = pack(done).reshape(SEQ, NA, 2 * C)
        send_back(t, ta, ra, 0)
        whole(rb.at[t], rr_sem.at[1, t])
        came = unpack(rb[t].reshape(SEQ * NB, 2 * C))[:, :C].astype(BF16)
        xs[t, ROWS_A:] = came
        came = jnp.where(section == 0, inc[plan[t], ROWS_A:], came)
        xi[ROWS_A:] = came
        pivot[...] = find_pivot(widen(came.astype(F32)), groups[...])
        whole(ra.at[t], rr_sem.at[0, t])
        came = unpack(ra[t].reshape(SEQ * NA, 2 * C))[:, :C].astype(BF16)
        xs[t, 0:ROWS_A] = came

        @pl.when(t < TICKS - 1)
        def _():
            pltpu.make_async_remote_copy(
                xs.at[t], out_ref.at[t], os_sem.at[t], or_sem.at[t],
                device_id={"section": prv, "seq": me}, device_id_type=MESH).start()
            xi[0:ROWS_A] = jnp.where(section == 0, inc[plan[t], 0:ROWS_A], xs[t, 0:ROWS_A])

        return carry

    lax.fori_loop(0, TICKS, tick, 0)
    out_ref[TICKS - 1] = xs[TICKS - 1]
    for t in range(TICKS):
        for lane, (src, back) in enumerate(((sa, ta), (sb, tb))):
            part = src.at[t, pl.ds(0, SEQ - 1)]
            pltpu.make_async_copy(part, part, fs_sem.at[lane, t]).wait()
            part = back.at[t, pl.ds(0, SEQ - 1 if t == TICKS - 1 else SEQ)]
            pltpu.make_async_copy(part, part, rs_sem.at[lane, t]).wait()
    for t in range(TICKS - 1):
        pltpu.make_async_copy(xs.at[t], xs.at[t], os_sem.at[t]).wait()
        pltpu.make_async_copy(out_ref.at[t], out_ref.at[t], or_sem.at[t]).wait()


def shards(incoming, plan, waiting, spatial_weight, temporal_weight, attn_in, attn_out):
    hbm = pl.BlockSpec(memory_space=pl.ANY)
    steps = (TICKS,)
    out = pl.pallas_call(
        body,
        out_shape=pltpu.VMEM((TICKS, CELLS, C), BF16),
        in_specs=[hbm, pl.BlockSpec(memory_space=pltpu.SMEM), hbm, hbm, hbm, hbm, hbm],
        out_specs=pl.BlockSpec(memory_space=pltpu.VMEM),
        scratch_shapes=[
            pltpu.VMEM((4, CELLS, C), BF16),
            pltpu.VMEM((CELLS, C), BF16),
            pltpu.VMEM(steps + (CELLS, C), BF16),
            pltpu.VMEM((2, 9, C, C), BF16),
            pltpu.VMEM((2, 3, C, C), BF16),
            pltpu.VMEM((C, 3 * C), BF16),
            pltpu.VMEM((C, C), BF16),
            pltpu.VMEM((2, DEEP, DEEP), BF16),
            pltpu.VMEM((2, DEEP, CP), BF16),
            pltpu.VMEM((CP, DEEP), BF16),
            pltpu.VMEM((CP, CP), BF16),
            pltpu.VMEM((CP, CP), BF16),
            pltpu.VMEM((1, CP), F32),
            pltpu.VMEM((BLOCK, BLOCK), F32),
            pltpu.VMEM((BLOCK, BLOCK), F32),
            pltpu.VMEM((CELLS, DEEP), BF16),
        ]
        + [pltpu.VMEM(steps + (SEQ, n, 2 * C), BF16) for _ in range(4) for n in (NA, NB)]
        + [
            pltpu.SemaphoreType.DMA((7,)),
            pltpu.SemaphoreType.DMA((2, TICKS)),
            pltpu.SemaphoreType.DMA((2, TICKS)),
            pltpu.SemaphoreType.DMA((2, TICKS)),
            pltpu.SemaphoreType.DMA((2, TICKS)),
            pltpu.SemaphoreType.DMA((TICKS - 1,)),
            pltpu.SemaphoreType.DMA((TICKS - 1,)),
            pltpu.SemaphoreType.REGULAR,
        ],
        compiler_params=pltpu.CompilerParams(
            collective_id=0, has_side_effects=True, vmem_limit_bytes=60 * 1024 * 1024),
    )(
        incoming.reshape(4, CELLS, C), plan, waiting.reshape(CELLS, C),
        spatial_weight[0], temporal_weight[0], attn_in[0], attn_out[0],
    )
    return out.reshape(TICKS, 1, 1, H, W, C)


def solution(mesh):
    return jax.shard_map(
        shards,
        mesh=mesh,
        in_specs=(
            P(None, "seq", None, None, None),
            P(),
            P("section", "seq", None, None, None),
            P("section", None, None, None, None),
            P("section", None, None, None, None),
            P("section", None, None),
            P("section", None, None),
        ),
        out_specs=P(None, "section", "seq", None, None, None),
        check_vma=False,
    )
```

```python
import jax
import jax.numpy as jnp
from jax import lax
from jax.experimental import pallas as pl
from jax.experimental.pallas import tpu as pltpu
from jax.sharding import PartitionSpec as P

TICKS = 3
SEQ = 32
NY = 4
NZ = 8
SECTIONS = 8
EPSILON = 1e-05
C = 320
CM = 256
CT = 64
CP = 384
LANES = 128
DEEP = 1024
W = 24
H = 16
CELLS = H * W
NA = 4
NB = 2
ROWS_A = SEQ * NA * 2
ROWS_B = SEQ * NB * 2
BLOCK = 128
PIVOT = ROWS_A
FAR = -1e30
MESH = pl.DeviceIdType.MESH
F32 = jnp.float32
BF16 = jnp.bfloat16


def hops(offset):
    dz, dy = offset
    return min(dz, NZ - dz) + min(dy, NY - dy)


OFFSETS = sorted(
    [(dz, dy) for dz in range(NZ) for dy in range(NY) if (dz, dy) != (0, 0)], key=lambda o: -hops(o)
)


def dot(a, b):
    return jnp.dot(a, b, preferred_element_type=F32)


def in_low(rows):
    return lax.broadcasted_iota(jnp.int32, (rows, LANES), 1) < CT


def turn(v):
    return pltpu.roll(v, CT, 1)


def widen(v):
    return jnp.concatenate([v, jnp.zeros((v.shape[0], CP - C), v.dtype)], axis=1)


def silu_of_half(h):
    return h * jnp.tanh(h) + h


def layer_norm(v, factor):
    center = jnp.sum(v, axis=-1, keepdims=True) * (1.0 / C)
    side = jnp.where(in_low(v.shape[0]), v[:, CM:] - center, 0.0)
    d = jnp.concatenate([v[:, :CM] - center, side], axis=1)
    spread = jnp.sum(d * d, axis=-1, keepdims=True) * (1.0 / C)
    return d * (factor * lax.rsqrt(spread + EPSILON))


def over_groups(rows, groups):
    high = rows.astype(BF16).astype(F32)
    rest = rows - high
    mid = rest.astype(BF16).astype(F32)
    low = rest - mid
    parts = jnp.concatenate([high, mid, low, jnp.zeros_like(low)], axis=0).astype(BF16)
    got = dot(parts, groups)
    return got[0:2] + got[2:4] + got[4:6]


def find_pivot(v, groups):
    total = jnp.sum(v, axis=0, keepdims=True)
    return over_groups(jnp.concatenate([total, total], axis=0), groups)[0:1] * (1.0 / (v.shape[0] * 10))


def group_norm_half(v, pivot, groups):
    count = 1.0 / (CELLS * 10)
    d = v - pivot
    sums = jnp.concatenate([jnp.sum(d, axis=0, keepdims=True), jnp.sum(d * d, axis=0, keepdims=True)], axis=0)
    means = over_groups(sums, groups) * count
    shift = means[0:1]
    spread = jnp.maximum(means[1:2] - shift * shift, 0.0)
    scale = 0.5 * lax.rsqrt(spread + EPSILON)
    return d * scale - shift * scale


def fill_taps(y, x_ref):
    main = y[:, :CM].astype(BF16)
    x_ref[W:, 0:CM] = main[: CELLS - W]
    x_ref[:, CM : 2 * CM] = main
    x_ref[: CELLS - W, 2 * CM : 3 * CM] = main[W:]
    tail = y[:, CM:]
    edge = jnp.zeros((W, LANES), F32)
    above = jnp.concatenate([edge, tail[: CELLS - W]], axis=0)
    below = jnp.concatenate([tail[W:], edge], axis=0)
    x_ref[:, 3 * CM : 3 * CM + LANES] = (above + turn(tail)).astype(BF16)
    x_ref[:, 3 * CM + LANES :] = below.astype(BF16)


def column_taps(p):
    rows = p.shape[0]
    high = rows // W

    def add(left, mid, right):
        width = left.shape[1]
        col = lax.broadcasted_iota(jnp.int32, (high, W, width), 1)
        left = pltpu.roll(left, 1, 0).reshape(high, W, width)
        right = pltpu.roll(right, rows - 1, 0).reshape(high, W, width)
        left = jnp.where(col > 0, left, 0.0).reshape(rows, width)
        right = jnp.where(col < W - 1, right, 0.0).reshape(rows, width)
        return mid + left + right

    main = add(p[:, 0:CM], p[:, CM : 2 * CM], p[:, 2 * CM : 3 * CM])
    pair = p[:, 3 * CM : 3 * CM + LANES]
    tail = jnp.where(in_low(rows), add(pair, turn(pair), p[:, 3 * CM + LANES :]), 0.0)
    return jnp.concatenate([main, tail], axis=1)


def pack(v):
    half = v.shape[0] // 2
    low, high = v[:half], v[half:]
    return jnp.concatenate([low[:, :CM], high[:, :CM], low[:, CM:] + turn(high[:, CM:])], axis=1).astype(BF16)


def unpack(p):
    p = p.astype(F32)
    side = p[:, 2 * CM :]
    mask = in_low(p.shape[0])
    low = jnp.concatenate([p[:, :CM], jnp.where(mask, side, 0.0)], axis=1)
    high = jnp.concatenate([p[:, CM : 2 * CM], jnp.where(mask, turn(side), 0.0)], axis=1)
    return jnp.concatenate([low, high], axis=0)


def temporal_taps(act, cells, half):
    rows = act.shape[0]
    row = lax.broadcasted_iota(jnp.int32, act.shape, 0) & (half - 1)
    before = jnp.where(row >= cells, pltpu.roll(act, cells, 0), 0.0)
    after = jnp.where(row < half - cells, pltpu.roll(act, rows - cells, 0), 0.0)
    return jnp.concatenate(
        [before[:, :CM], act[:, :CM], after[:, :CM], before[:, CM:] + turn(act[:, CM:]), after[:, CM:]], axis=1
    ).astype(BF16)


def attention(proj, bias):
    low = in_low(BLOCK)
    scale = 0.125 * 1.4426950408889634
    scores, held = [], []
    for pair in range(3):
        q = proj[:, 128 * pair : 128 * pair + 128]
        k = proj[:, 384 + 128 * pair : 512 + 128 * pair].astype(BF16)
        v = (proj[:, 768 + 128 * pair : 896 + 128 * pair] if pair < 2 else turn(q)).T.astype(BF16)
        for side in range(2 if pair < 2 else 1):
            own = low if side == 0 else jnp.logical_not(low)
            one = jnp.where(own, q, 0.0).astype(BF16)
            scores.append(lax.dot_general(k, one, (((1,), (1,)), ((), ())), preferred_element_type=F32) + bias)
            held.append(v[CT * side : CT * side + CT])
    tops = [jnp.max(s, axis=0, keepdims=True) for s in scores]
    weights = [jnp.exp2((s - top) * scale) for s, top in zip(scores, tops)]
    totals = [jnp.sum(w, axis=0, keepdims=True) for w in weights]
    mixed = [dot(v, w.astype(BF16)) * (1.0 / total) for v, w, total in zip(held, weights, totals)]
    return jnp.concatenate(mixed + [jnp.zeros((CT, BLOCK), F32)], axis=0).T.astype(BF16)


def temporal_part(x1, cells, tw_ref, wi_ref, wo_ref, bias_ref):
    half = x1.shape[0] // 2
    bias = bias_ref[...]
    x1 = [x1[at : at + BLOCK] for at in range(0, 2 * half, BLOCK)]
    taps = [temporal_taps(silu_of_half(layer_norm(v, 0.5)), cells, half) for v in x1]
    u = [dot(v, tw_ref[0]).astype(BF16).astype(F32) for v in taps]
    taps = [temporal_taps(silu_of_half(layer_norm(v, 0.5)), cells, half) for v in u]
    x2 = [(v + dot(tap, tw_ref[1])).astype(BF16).astype(F32) for v, tap in zip(x1, taps)]
    normed = [layer_norm(v, 1.0).astype(BF16) for v in x2]
    proj = [dot(v, wi_ref[...]) for v in normed]
    mixed = [attention(v, bias) for v in proj]
    done = [v + dot(mix, wo_ref[...]) for v, mix in zip(x2, mixed)]
    return done[0] if len(done) == 1 else jnp.concatenate(done, axis=0)


def body(
    inc_hbm, plan_hbm, wait_hbm, sw_hbm, tw_hbm, ai_hbm, ao_hbm, out_ref,
    plan, inc, xi, xs, sw, tws, ai, ao, wc, tw, wi, wo, groups, pivot, bias_a, bias_b, taps,
    sa, sb, fa, fb, ta, tb, ra, rb,
    in_sem, fs_sem, fr_sem, rs_sem, rr_sem, os_sem, or_sem, ready,
):
    me = lax.axis_index("seq")
    section = lax.axis_index("section")
    nxt = lax.rem(section + 1, SECTIONS)
    prv = lax.rem(section + SECTIONS - 1, SECTIONS)
    my_z = me // NY
    my_y = lax.rem(me, NY)

    def peer(offset):
        dz, dy = offset
        return lax.rem(my_z + dz, NZ) * NY + lax.rem(my_y + dy, NY)

    loads = [
        pltpu.make_async_copy(wait_hbm, xi, in_sem.at[0]),
        pltpu.make_async_copy(sw_hbm.at[0], sw.at[0], in_sem.at[1]),
        pltpu.make_async_copy(sw_hbm.at[1], sw.at[1], in_sem.at[2]),
        pltpu.make_async_copy(ai_hbm, ai, in_sem.at[3]),
        pltpu.make_async_copy(ao_hbm, ao, in_sem.at[4]),
        pltpu.make_async_copy(inc_hbm, inc, in_sem.at[5]),
    ]
    loads.append(pltpu.make_async_copy(tw_hbm, tws, in_sem.at[6]))
    loads.append(pltpu.make_async_copy(plan_hbm, plan, in_sem.at[7]))
    for load in loads[:3]:
        load.start()

    barrier = pltpu.get_barrier_semaphore()
    for offset in OFFSETS:
        pl.semaphore_signal(barrier, 1, device_id={"section": section, "seq": peer(offset)}, device_id_type=MESH)
    for other in (nxt, prv):
        pl.semaphore_signal(barrier, 1, device_id={"section": other, "seq": me}, device_id_type=MESH)

    for load in loads[3:]:
        load.start()

    row = lax.broadcasted_iota(jnp.int32, (CP, CP), 0)
    col = lax.broadcasted_iota(jnp.int32, (CP, CP), 1)
    groups[...] = jnp.where(((row * 6554) // 65536 == (col * 6554) // 65536) & (row < C), 1.0, 0.0).astype(BF16)
    taps[0:W, 0:CM] = jnp.zeros((W, CM), BF16)
    taps[CELLS - W :, 2 * CM : 3 * CM] = jnp.zeros((W, CM), BF16)

    def make_bias():
        r = lax.broadcasted_iota(jnp.int32, (BLOCK, BLOCK), 0)
        c = lax.broadcasted_iota(jnp.int32, (BLOCK, BLOCK), 1)
        bias_a[...] = jnp.where((r & (NA - 1)) == (c & (NA - 1)), 0.0, FAR)
        half = SEQ * NB
        same = ((r & (NB - 1)) == (c & (NB - 1))) & ((r & half) == (c & half))
        bias_b[...] = jnp.where(same, 0.0, FAR)

    def pack_conv(k):
        for i in range(3):
            part = [widen(sw[k, 3 * i + j]) for j in range(3)]
            side = [t[:, CM:].astype(F32) for t in part]
            whole = jnp.concatenate(
                [t[:, :CM] for t in part] + [(side[0] + turn(side[1])).astype(BF16), part[2][:, CM:]], axis=1)
            wc[k, CM * i : CM * i + CM] = whole[:CM]
            wc[k, 3 * CM + CT * i : 3 * CM + CT * i + CT] = whole[CM:]
        wc[k, 3 * C :] = jnp.zeros((DEEP - 3 * C, DEEP), BF16)

    def pack_temporal():
        for k in range(2):
            for i in range(3):
                part = widen(tws[k, i])
                tw[k, CM * i : CM * i + CM] = part[:CM]
                tw[k, 3 * CM + CT * i : 3 * CM + CT * i + CT] = part[CM:]
            tw[k, 3 * C :] = jnp.zeros((DEEP - 3 * C, CP), BF16)

    def pack_attn():
        whole = ai[...].astype(F32)
        cross = whole[:, 256:384]
        mid = whole[:, 384:640]
        last = jnp.concatenate([whole[:, 896:960], jnp.zeros((C, CT), F32)], axis=1)
        low = in_low(C)
        turned = [turn(t) for t in (cross, mid[:, :128], mid[:, 128:])]
        wi[:C, 0:256] = ai[:, :256]
        wi[:C, 256:384] = jnp.where(low, cross, turn(last)).astype(BF16)
        wi[:C, 384:512] = jnp.where(low, turned[0], turned[1]).astype(BF16)
        wi[:C, 512:640] = jnp.where(low, turned[1], turned[2]).astype(BF16)
        wi[:C, 640:768] = jnp.where(low, turned[2], 0.0).astype(BF16)
        wi[:C, 768:1024] = ai[:, 640:896]
        wi[C:] = jnp.zeros((CP - C, DEEP), BF16)
        wo[:C] = widen(ao[...])
        wo[C:] = jnp.zeros((CP - C, CP), BF16)

    def send_all(t, src, dst, to_section, send_sem, recv_sem):
        for offset in OFFSETS:
            to = peer(offset)
            pltpu.make_async_remote_copy(
                src.at[t, to], dst.at[t, me], send_sem, recv_sem,
                device_id={"section": to_section, "seq": to}, device_id_type=MESH).start()

    def send_forward(t, src, dst, lane):
        send_all(t, src, dst, section, fs_sem.at[lane, t], fr_sem.at[lane, t])
        pltpu.make_async_copy(src.at[t, me], dst.at[t, me], fr_sem.at[lane, t]).start()

    def send_back(t, src, dst, lane):
        if t == TICKS - 1:
            send_all(t, src, dst, section, rs_sem.at[lane, t], rr_sem.at[lane, t])
            pltpu.make_async_copy(src.at[t, me], dst.at[t, me], rr_sem.at[lane, t]).start()
        else:
            send_all(t, src, dst, nxt, rs_sem.at[lane, t], rr_sem.at[lane, t])
            pltpu.make_async_remote_copy(
                src.at[t, me], dst.at[t, me], rs_sem.at[lane, t], rr_sem.at[lane, t],
                device_id={"section": nxt, "seq": me}, device_id_type=MESH).start()

    def whole(ref, sem):
        pltpu.make_async_copy(ref, ref, sem).wait()

    loads[0].wait()
    pivot[...] = find_pivot(widen(xi[ROWS_A:].astype(F32)), groups[...])
    top = 11 * W
    for t in range(TICKS):
        x = widen(xi[...].astype(F32))
        fill_taps(silu_of_half(group_norm_half(x, pivot[...], groups[...])), taps)
        if t == 0:
            loads[1].wait()
            pack_conv(0)
        p = dot(taps[...], wc[0])
        if t == 0:
            loads[2].wait()
            pack_conv(1)
        a = column_taps(p).astype(BF16).astype(F32)
        fill_taps(silu_of_half(group_norm_half(a, find_pivot(a[:PIVOT], groups[...]), groups[...])), taps)
        got = column_taps(dot(taps[top - W :], wc[1]))
        sb[t] = pack(x[ROWS_A:] + got[ROWS_A - top + W :]).reshape(SEQ, NB, 2 * C)
        if t == 0:
            pl.semaphore_wait(barrier, SEQ + 1)
        send_forward(t, sb, fb, 1)
        got = column_taps(dot(taps[0:top], wc[1]))
        sa[t] = pack(x[:ROWS_A] + got[:ROWS_A]).reshape(SEQ, NA, 2 * C)
        send_forward(t, sa, fa, 0)
        if t == 0:
            make_bias()
            for load in loads[3:]:
                load.wait()
            pack_temporal()
            pack_attn()

        whole(fb.at[t], fr_sem.at[1, t])
        if t == 0:
            pl.semaphore_signal(ready, 1, device_id={"section": prv, "seq": me}, device_id_type=MESH)
        done = temporal_part(unpack(fb[t].reshape(SEQ * NB, 2 * C)), NB, tw, wi, wo, bias_b)
        tb[t] = pack(done).reshape(SEQ, NB, 2 * C)
        if t == 0:
            pl.semaphore_wait(ready, 1)
        send_back(t, tb, rb, 1)
        whole(fa.at[t], fr_sem.at[0, t])
        done = temporal_part(unpack(fa[t].reshape(SEQ * NA, 2 * C)), NA, tw, wi, wo, bias_a)
        ta[t] = pack(done).reshape(SEQ, NA, 2 * C)
        send_back(t, ta, ra, 0)

        whole(rb.at[t], rr_sem.at[1, t])
        came_b = unpack(rb[t].reshape(SEQ * NB, 2 * C))[:, :C].astype(BF16)
        if t == TICKS - 1:
            out_ref[t, ROWS_A:] = came_b
            whole(ra.at[t], rr_sem.at[0, t])
            out_ref[t, 0:ROWS_A] = unpack(ra[t].reshape(SEQ * NA, 2 * C))[:, :C].astype(BF16)
            break
        xs[t, ROWS_A:] = came_b
        came_b = jnp.where(section == 0, inc[plan[t], ROWS_A:], came_b)
        xi[ROWS_A:] = came_b
        pivot[...] = find_pivot(widen(came_b.astype(F32)), groups[...])
        whole(ra.at[t], rr_sem.at[0, t])
        came_a = unpack(ra[t].reshape(SEQ * NA, 2 * C))[:, :C].astype(BF16)
        xs[t, 0:ROWS_A] = came_a
        xi[0:ROWS_A] = jnp.where(section == 0, inc[plan[t], 0:ROWS_A], came_a)
        pltpu.make_async_remote_copy(
            xs.at[t], out_ref.at[t], os_sem.at[t], or_sem.at[t],
            device_id={"section": prv, "seq": me}, device_id_type=MESH).start()

    for t in range(TICKS):
        for lane, (src, back) in enumerate(((sa, ta), (sb, tb))):
            part = src.at[t, pl.ds(0, SEQ - 1)]
            pltpu.make_async_copy(part, part, fs_sem.at[lane, t]).wait()
            part = back.at[t, pl.ds(0, SEQ - 1 if t == TICKS - 1 else SEQ)]
            pltpu.make_async_copy(part, part, rs_sem.at[lane, t]).wait()
    for t in range(TICKS - 1):
        pltpu.make_async_copy(xs.at[t], xs.at[t], os_sem.at[t]).wait()
        pltpu.make_async_copy(out_ref.at[t], out_ref.at[t], or_sem.at[t]).wait()


def shards(incoming, plan, waiting, spatial_weight, temporal_weight, attn_in, attn_out):
    hbm = pl.BlockSpec(memory_space=pl.ANY)
    steps = (TICKS,)
    out = pl.pallas_call(
        body,
        out_shape=pltpu.VMEM((TICKS, CELLS, C), BF16),
        in_specs=[hbm] * 7,
        out_specs=pl.BlockSpec(memory_space=pltpu.VMEM),
        scratch_shapes=[
            pltpu.SMEM((4,), jnp.int32),
            pltpu.VMEM((4, CELLS, C), BF16),
            pltpu.VMEM((CELLS, C), BF16),
            pltpu.VMEM((TICKS - 1, CELLS, C), BF16),
            pltpu.VMEM((2, 9, C, C), BF16),
            pltpu.VMEM((2, 3, C, C), BF16),
            pltpu.VMEM((C, 3 * C), BF16),
            pltpu.VMEM((C, C), BF16),
            pltpu.VMEM((2, DEEP, DEEP), BF16),
            pltpu.VMEM((2, DEEP, CP), BF16),
            pltpu.VMEM((CP, DEEP), BF16),
            pltpu.VMEM((CP, CP), BF16),
            pltpu.VMEM((CP, CP), BF16),
            pltpu.VMEM((1, CP), F32),
            pltpu.VMEM((BLOCK, BLOCK), F32),
            pltpu.VMEM((BLOCK, BLOCK), F32),
            pltpu.VMEM((CELLS, DEEP), BF16),
        ]
        + [pltpu.VMEM(steps + (SEQ, n, 2 * C), BF16) for _ in range(4) for n in (NA, NB)]
        + [
            pltpu.SemaphoreType.DMA((8,)),
            pltpu.SemaphoreType.DMA((2, TICKS)),
            pltpu.SemaphoreType.DMA((2, TICKS)),
            pltpu.SemaphoreType.DMA((2, TICKS)),
            pltpu.SemaphoreType.DMA((2, TICKS)),
            pltpu.SemaphoreType.DMA((TICKS - 1,)),
            pltpu.SemaphoreType.DMA((TICKS - 1,)),
            pltpu.SemaphoreType.REGULAR,
        ],
        compiler_params=pltpu.CompilerParams(
            collective_id=0, has_side_effects=True, vmem_limit_bytes=60 * 1024 * 1024),
    )(
        incoming.reshape(4, CELLS, C), plan, waiting.reshape(CELLS, C),
        spatial_weight[0], temporal_weight[0], attn_in[0], attn_out[0],
    )
    return out.reshape(TICKS, 1, 1, H, W, C)


def solution(mesh):
    return jax.shard_map(
        shards,
        mesh=mesh,
        in_specs=(
            P(None, "seq", None, None, None),
            P(),
            P("section", "seq", None, None, None),
            P("section", None, None, None, None),
            P("section", None, None, None, None),
            P("section", None, None),
            P("section", None, None),
        ),
        out_specs=P(None, "section", "seq", None, None, None),
        check_vma=False,
    )
```

```python
import jax
import jax.numpy as jnp
from jax import lax
from jax.experimental import pallas as pl
from jax.experimental.pallas import tpu as pltpu
from jax.sharding import PartitionSpec as P

TICKS = 3
SEQ = 32
NY = 4
NZ = 8
SECTIONS = 8
EPSILON = 1e-05
C = 320
CM = 256
CT = 64
CP = 384
LANES = 128
DEEP = 1024
W = 24
H = 16
CELLS = H * W
NA = 4
NB = 2
ROWS_A = SEQ * NA * 2
ROWS_B = SEQ * NB * 2
BLOCK = 128
PIVOT = 2 * W
FAR = -1e30
MESH = pl.DeviceIdType.MESH
F32 = jnp.float32
BF16 = jnp.bfloat16


def hops(offset):
    dz, dy = offset
    return min(dz, NZ - dz) + min(dy, NY - dy)


OFFSETS = sorted(
    [(dz, dy) for dz in range(NZ) for dy in range(NY) if (dz, dy) != (0, 0)], key=lambda o: -hops(o)
)


def dot(a, b):
    return jnp.dot(a, b, preferred_element_type=F32)


def in_low(rows):
    return lax.broadcasted_iota(jnp.int32, (rows, LANES), 1) < CT


def turn(v):
    return pltpu.roll(v, CT, 1)


def widen(v):
    return jnp.concatenate([v, jnp.zeros((v.shape[0], CP - C), v.dtype)], axis=1)


def silu_of_half(h):
    return h * jnp.tanh(h) + h


def layer_norm(v, factor):
    center = jnp.sum(v, axis=-1, keepdims=True) * (1.0 / C)
    side = jnp.where(in_low(v.shape[0]), v[:, CM:] - center, 0.0)
    d = jnp.concatenate([v[:, :CM] - center, side], axis=1)
    spread = jnp.sum(d * d, axis=-1, keepdims=True) * (1.0 / C)
    return d * (factor * lax.rsqrt(spread + EPSILON))


def over_groups(rows, groups):
    high = rows.astype(BF16).astype(F32)
    rest = rows - high
    mid = rest.astype(BF16).astype(F32)
    low = rest - mid
    parts = jnp.concatenate([high, mid, low, jnp.zeros_like(low)], axis=0).astype(BF16)
    got = dot(parts, groups)
    return got[0:2] + got[2:4] + got[4:6]


def find_pivot(v, groups):
    total = jnp.sum(v, axis=0, keepdims=True)
    return over_groups(jnp.concatenate([total, total], axis=0), groups)[0:1] * (1.0 / (v.shape[0] * 10))


def group_norm_half(v, pivot, groups):
    count = 1.0 / (CELLS * 10)
    d = v - pivot
    sums = jnp.concatenate([jnp.sum(d, axis=0, keepdims=True), jnp.sum(d * d, axis=0, keepdims=True)], axis=0)
    means = over_groups(sums, groups) * count
    shift = means[0:1]
    spread = jnp.maximum(means[1:2] - shift * shift, 0.0)
    scale = 0.5 * lax.rsqrt(spread + EPSILON)
    return d * scale - shift * scale


def fill_taps(y, x_ref):
    main = y[:, :CM].astype(BF16)
    x_ref[W:, 0:CM] = main[: CELLS - W]
    x_ref[:, CM : 2 * CM] = main
    x_ref[: CELLS - W, 2 * CM : 3 * CM] = main[W:]
    tail = y[:, CM:]
    edge = jnp.zeros((W, LANES), F32)
    above = jnp.concatenate([edge, tail[: CELLS - W]], axis=0)
    below = jnp.concatenate([tail[W:], edge], axis=0)
    x_ref[:, 3 * CM : 3 * CM + LANES] = (above + turn(tail)).astype(BF16)
    x_ref[:, 3 * CM + LANES :] = below.astype(BF16)


def column_taps(p):
    rows = p.shape[0]
    high = rows // W

    def add(left, mid, right):
        width = left.shape[1]
        col = lax.broadcasted_iota(jnp.int32, (high, W, width), 1)
        left = pltpu.roll(left, 1, 0).reshape(high, W, width)
        right = pltpu.roll(right, rows - 1, 0).reshape(high, W, width)
        left = jnp.where(col > 0, left, 0.0).reshape(rows, width)
        right = jnp.where(col < W - 1, right, 0.0).reshape(rows, width)
        return mid + left + right

    main = add(p[:, 0:CM], p[:, CM : 2 * CM], p[:, 2 * CM : 3 * CM])
    pair = p[:, 3 * CM : 3 * CM + LANES]
    tail = jnp.where(in_low(rows), add(pair, turn(pair), p[:, 3 * CM + LANES :]), 0.0)
    return jnp.concatenate([main, tail], axis=1)


def pack(v):
    half = v.shape[0] // 2
    low, high = v[:half], v[half:]
    return jnp.concatenate([low[:, :CM], high[:, :CM], low[:, CM:] + turn(high[:, CM:])], axis=1).astype(BF16)


def unpack(p):
    p = p.astype(F32)
    side = p[:, 2 * CM :]
    mask = in_low(p.shape[0])
    low = jnp.concatenate([p[:, :CM], jnp.where(mask, side, 0.0)], axis=1)
    high = jnp.concatenate([p[:, CM : 2 * CM], jnp.where(mask, turn(side), 0.0)], axis=1)
    return jnp.concatenate([low, high], axis=0)


def temporal_taps(act, cells, half):
    rows = act.shape[0]
    row = lax.broadcasted_iota(jnp.int32, act.shape, 0) & (half - 1)
    before = jnp.where(row >= cells, pltpu.roll(act, cells, 0), 0.0)
    after = jnp.where(row < half - cells, pltpu.roll(act, rows - cells, 0), 0.0)
    return jnp.concatenate(
        [before[:, :CM], act[:, :CM], after[:, :CM], before[:, CM:] + turn(act[:, CM:]), after[:, CM:]], axis=1
    ).astype(BF16)


def attention(proj, bias):
    low = in_low(BLOCK)
    scale = 0.125 * 1.4426950408889634
    scores, held = [], []
    for pair in range(3):
        q = proj[:, 128 * pair : 128 * pair + 128]
        k = proj[:, 384 + 128 * pair : 512 + 128 * pair].astype(BF16)
        v = (proj[:, 768 + 128 * pair : 896 + 128 * pair] if pair < 2 else turn(q)).T.astype(BF16)
        for side in range(2 if pair < 2 else 1):
            own = low if side == 0 else jnp.logical_not(low)
            one = jnp.where(own, q, 0.0).astype(BF16)
            scores.append(lax.dot_general(k, one, (((1,), (1,)), ((), ())), preferred_element_type=F32) + bias)
            held.append(v[CT * side : CT * side + CT])
    tops = [jnp.max(s, axis=0, keepdims=True) for s in scores]
    weights = [jnp.exp2((s - top) * scale) for s, top in zip(scores, tops)]
    totals = [jnp.sum(w, axis=0, keepdims=True) for w in weights]
    mixed = [dot(v, w.astype(BF16)) * (1.0 / total) for v, w, total in zip(held, weights, totals)]
    return jnp.concatenate(mixed + [jnp.zeros((CT, BLOCK), F32)], axis=0).T.astype(BF16)


def temporal_part(x1, cells, tw_ref, wi_ref, wo_ref, bias_ref):
    half = x1.shape[0] // 2
    bias = bias_ref[...]
    x1 = [x1[at : at + BLOCK] for at in range(0, 2 * half, BLOCK)]
    taps = [temporal_taps(silu_of_half(layer_norm(v, 0.5)), cells, half) for v in x1]
    u = [dot(v, tw_ref[0]).astype(BF16).astype(F32) for v in taps]
    taps = [temporal_taps(silu_of_half(layer_norm(v, 0.5)), cells, half) for v in u]
    x2 = [(v + dot(tap, tw_ref[1])).astype(BF16).astype(F32) for v, tap in zip(x1, taps)]
    normed = [layer_norm(v, 1.0).astype(BF16) for v in x2]
    proj = [dot(v, wi_ref[...]) for v in normed]
    mixed = [attention(v, bias) for v in proj]
    done = [v + dot(mix, wo_ref[...]) for v, mix in zip(x2, mixed)]
    return done[0] if len(done) == 1 else jnp.concatenate(done, axis=0)


def body(
    inc_hbm, plan_hbm, wait_hbm, sw_hbm, tw_hbm, ai_hbm, ao_hbm, out_ref,
    plan, inc, xi, xs, sw, tws, ai, ao, wc, tw, wi, wo, groups, pivot, bias_a, bias_b, taps,
    sa, sb, fa, fb, ta, tb, ra, rb,
    in_sem, fs_sem, fr_sem, rs_sem, rr_sem, os_sem, or_sem, ready,
):
    me = lax.axis_index("seq")
    section = lax.axis_index("section")
    nxt = lax.rem(section + 1, SECTIONS)
    prv = lax.rem(section + SECTIONS - 1, SECTIONS)
    my_z = me // NY
    my_y = lax.rem(me, NY)

    def peer(offset):
        dz, dy = offset
        return lax.rem(my_z + dz, NZ) * NY + lax.rem(my_y + dy, NY)

    loads = [
        pltpu.make_async_copy(wait_hbm, xi, in_sem.at[0]),
        pltpu.make_async_copy(sw_hbm.at[0], sw.at[0], in_sem.at[1]),
        pltpu.make_async_copy(sw_hbm.at[1], sw.at[1], in_sem.at[2]),
        pltpu.make_async_copy(ai_hbm, ai, in_sem.at[3]),
        pltpu.make_async_copy(ao_hbm, ao, in_sem.at[4]),
        pltpu.make_async_copy(inc_hbm, inc, in_sem.at[5]),
    ]
    loads.append(pltpu.make_async_copy(tw_hbm, tws, in_sem.at[6]))
    loads.append(pltpu.make_async_copy(plan_hbm, plan, in_sem.at[7]))
    for load in loads[:3]:
        load.start()

    barrier = pltpu.get_barrier_semaphore()
    for offset in OFFSETS:
        pl.semaphore_signal(barrier, 1, device_id={"section": section, "seq": peer(offset)}, device_id_type=MESH)
    for other in (nxt, prv):
        pl.semaphore_signal(barrier, 1, device_id={"section": other, "seq": me}, device_id_type=MESH)

    for load in loads[3:]:
        load.start()

    row = lax.broadcasted_iota(jnp.int32, (CP, CP), 0)
    col = lax.broadcasted_iota(jnp.int32, (CP, CP), 1)
    groups[...] = jnp.where(((row * 6554) // 65536 == (col * 6554) // 65536) & (row < C), 1.0, 0.0).astype(BF16)
    taps[0:W, 0:CM] = jnp.zeros((W, CM), BF16)
    taps[CELLS - W :, 2 * CM : 3 * CM] = jnp.zeros((W, CM), BF16)

    def make_bias():
        r = lax.broadcasted_iota(jnp.int32, (BLOCK, BLOCK), 0)
        c = lax.broadcasted_iota(jnp.int32, (BLOCK, BLOCK), 1)
        bias_a[...] = jnp.where((r & (NA - 1)) == (c & (NA - 1)), 0.0, FAR)
        half = SEQ * NB
        same = ((r & (NB - 1)) == (c & (NB - 1))) & ((r & half) == (c & half))
        bias_b[...] = jnp.where(same, 0.0, FAR)

    def pack_conv(k):
        for i in range(3):
            part = [widen(sw[k, 3 * i + j]) for j in range(3)]
            side = [t[:, CM:].astype(F32) for t in part]
            whole = jnp.concatenate(
                [t[:, :CM] for t in part] + [(side[0] + turn(side[1])).astype(BF16), part[2][:, CM:]], axis=1)
            wc[k, CM * i : CM * i + CM] = whole[:CM]
            wc[k, 3 * CM + CT * i : 3 * CM + CT * i + CT] = whole[CM:]
        wc[k, 3 * C :] = jnp.zeros((DEEP - 3 * C, DEEP), BF16)

    def pack_temporal():
        for k in range(2):
            for i in range(3):
                part = widen(tws[k, i])
                tw[k, CM * i : CM * i + CM] = part[:CM]
                tw[k, 3 * CM + CT * i : 3 * CM + CT * i + CT] = part[CM:]
            tw[k, 3 * C :] = jnp.zeros((DEEP - 3 * C, CP), BF16)

    def pack_attn():
        whole = ai[...].astype(F32)
        cross = whole[:, 256:384]
        mid = whole[:, 384:640]
        last = jnp.concatenate([whole[:, 896:960], jnp.zeros((C, CT), F32)], axis=1)
        low = in_low(C)
        turned = [turn(t) for t in (cross, mid[:, :128], mid[:, 128:])]
        wi[:C, 0:256] = ai[:, :256]
        wi[:C, 256:384] = jnp.where(low, cross, turn(last)).astype(BF16)
        wi[:C, 384:512] = jnp.where(low, turned[0], turned[1]).astype(BF16)
        wi[:C, 512:640] = jnp.where(low, turned[1], turned[2]).astype(BF16)
        wi[:C, 640:768] = jnp.where(low, turned[2], 0.0).astype(BF16)
        wi[:C, 768:1024] = ai[:, 640:896]
        wi[C:] = jnp.zeros((CP - C, DEEP), BF16)
        wo[:C] = widen(ao[...])
        wo[C:] = jnp.zeros((CP - C, CP), BF16)

    def send_all(t, src, dst, to_section, send_sem, recv_sem):
        for offset in OFFSETS:
            to = peer(offset)
            pltpu.make_async_remote_copy(
                src.at[t, to], dst.at[t, me], send_sem, recv_sem,
                device_id={"section": to_section, "seq": to}, device_id_type=MESH).start()

    def send_forward(t, src, dst, lane):
        send_all(t, src, dst, section, fs_sem.at[lane, t], fr_sem.at[lane, t])
        pltpu.make_async_copy(src.at[t, me], dst.at[t, me], fr_sem.at[lane, t]).start()

    def send_back(t, src, dst, lane):
        if t == TICKS - 1:
            send_all(t, src, dst, section, rs_sem.at[lane, t], rr_sem.at[lane, t])
            pltpu.make_async_copy(src.at[t, me], dst.at[t, me], rr_sem.at[lane, t]).start()
        else:
            send_all(t, src, dst, nxt, rs_sem.at[lane, t], rr_sem.at[lane, t])
            pltpu.make_async_remote_copy(
                src.at[t, me], dst.at[t, me], rs_sem.at[lane, t], rr_sem.at[lane, t],
                device_id={"section": nxt, "seq": me}, device_id_type=MESH).start()

    def whole(ref, sem):
        pltpu.make_async_copy(ref, ref, sem).wait()

    loads[0].wait()
    pivot[...] = find_pivot(widen(xi[ROWS_A:].astype(F32)), groups[...])
    top = 11 * W
    for t in range(TICKS):
        x = widen(xi[...].astype(F32))
        fill_taps(silu_of_half(group_norm_half(x, pivot[...], groups[...])), taps)
        if t == 0:
            loads[1].wait()
            pack_conv(0)
        p = dot(taps[...], wc[0])
        if t == 0:
            loads[2].wait()
            pack_conv(1)
        a = column_taps(p).astype(BF16).astype(F32)
        fill_taps(silu_of_half(group_norm_half(a, find_pivot(a[:PIVOT], groups[...]), groups[...])), taps)
        got = column_taps(dot(taps[top - W :], wc[1]))
        sb[t] = pack(x[ROWS_A:] + got[ROWS_A - top + W :]).reshape(SEQ, NB, 2 * C)
        if t == 0:
            pl.semaphore_wait(barrier, SEQ + 1)
        send_forward(t, sb, fb, 1)
        got = column_taps(dot(taps[0:top], wc[1]))
        sa[t] = pack(x[:ROWS_A] + got[:ROWS_A]).reshape(SEQ, NA, 2 * C)
        send_forward(t, sa, fa, 0)
        if t == 0:
            make_bias()
            for load in loads[3:]:
                load.wait()
            pack_temporal()
            pack_attn()

        whole(fb.at[t], fr_sem.at[1, t])
        if t == 0:
            pl.semaphore_signal(ready, 1, device_id={"section": prv, "seq": me}, device_id_type=MESH)
        done = temporal_part(unpack(fb[t].reshape(SEQ * NB, 2 * C)), NB, tw, wi, wo, bias_b)
        tb[t] = pack(done).reshape(SEQ, NB, 2 * C)
        if t == 0:
            pl.semaphore_wait(ready, 1)
        send_back(t, tb, rb, 1)
        whole(fa.at[t], fr_sem.at[0, t])
        done = temporal_part(unpack(fa[t].reshape(SEQ * NA, 2 * C)), NA, tw, wi, wo, bias_a)
        ta[t] = pack(done).reshape(SEQ, NA, 2 * C)
        send_back(t, ta, ra, 0)

        whole(rb.at[t], rr_sem.at[1, t])
        came_b = unpack(rb[t].reshape(SEQ * NB, 2 * C))[:, :C].astype(BF16)
        if t == TICKS - 1:
            out_ref[t, ROWS_A:] = came_b
            whole(ra.at[t], rr_sem.at[0, t])
            out_ref[t, 0:ROWS_A] = unpack(ra[t].reshape(SEQ * NA, 2 * C))[:, :C].astype(BF16)
            break
        xs[t, ROWS_A:] = came_b
        came_b = jnp.where(section == 0, inc[plan[t], ROWS_A:], came_b)
        xi[ROWS_A:] = came_b
        pivot[...] = find_pivot(widen(came_b.astype(F32)), groups[...])
        whole(ra.at[t], rr_sem.at[0, t])
        came_a = unpack(ra[t].reshape(SEQ * NA, 2 * C))[:, :C].astype(BF16)
        xs[t, 0:ROWS_A] = came_a
        xi[0:ROWS_A] = jnp.where(section == 0, inc[plan[t], 0:ROWS_A], came_a)
        pltpu.make_async_remote_copy(
            xs.at[t], out_ref.at[t], os_sem.at[t], or_sem.at[t],
            device_id={"section": prv, "seq": me}, device_id_type=MESH).start()

    for t in range(TICKS):
        for lane, (src, back) in enumerate(((sa, ta), (sb, tb))):
            part = src.at[t, pl.ds(0, SEQ - 1)]
            pltpu.make_async_copy(part, part, fs_sem.at[lane, t]).wait()
            part = back.at[t, pl.ds(0, SEQ - 1 if t == TICKS - 1 else SEQ)]
            pltpu.make_async_copy(part, part, rs_sem.at[lane, t]).wait()
    for t in range(TICKS - 1):
        pltpu.make_async_copy(xs.at[t], xs.at[t], os_sem.at[t]).wait()
        pltpu.make_async_copy(out_ref.at[t], out_ref.at[t], or_sem.at[t]).wait()


def shards(incoming, plan, waiting, spatial_weight, temporal_weight, attn_in, attn_out):
    hbm = pl.BlockSpec(memory_space=pl.ANY)
    steps = (TICKS,)
    out = pl.pallas_call(
        body,
        out_shape=pltpu.VMEM((TICKS, CELLS, C), BF16),
        in_specs=[hbm] * 7,
        out_specs=pl.BlockSpec(memory_space=pltpu.VMEM),
        scratch_shapes=[
            pltpu.SMEM((4,), jnp.int32),
            pltpu.VMEM((4, CELLS, C), BF16),
            pltpu.VMEM((CELLS, C), BF16),
            pltpu.VMEM((TICKS - 1, CELLS, C), BF16),
            pltpu.VMEM((2, 9, C, C), BF16),
            pltpu.VMEM((2, 3, C, C), BF16),
            pltpu.VMEM((C, 3 * C), BF16),
            pltpu.VMEM((C, C), BF16),
            pltpu.VMEM((2, DEEP, DEEP), BF16),
            pltpu.VMEM((2, DEEP, CP), BF16),
            pltpu.VMEM((CP, DEEP), BF16),
            pltpu.VMEM((CP, CP), BF16),
            pltpu.VMEM((CP, CP), BF16),
            pltpu.VMEM((1, CP), F32),
            pltpu.VMEM((BLOCK, BLOCK), F32),
            pltpu.VMEM((BLOCK, BLOCK), F32),
            pltpu.VMEM((CELLS, DEEP), BF16),
        ]
        + [pltpu.VMEM(steps + (SEQ, n, 2 * C), BF16) for _ in range(4) for n in (NA, NB)]
        + [
            pltpu.SemaphoreType.DMA((8,)),
            pltpu.SemaphoreType.DMA((2, TICKS)),
            pltpu.SemaphoreType.DMA((2, TICKS)),
            pltpu.SemaphoreType.DMA((2, TICKS)),
            pltpu.SemaphoreType.DMA((2, TICKS)),
            pltpu.SemaphoreType.DMA((TICKS - 1,)),
            pltpu.SemaphoreType.DMA((TICKS - 1,)),
            pltpu.SemaphoreType.REGULAR,
        ],
        compiler_params=pltpu.CompilerParams(
            collective_id=0, has_side_effects=True, vmem_limit_bytes=60 * 1024 * 1024),
    )(
        incoming.reshape(4, CELLS, C), plan, waiting.reshape(CELLS, C),
        spatial_weight[0], temporal_weight[0], attn_in[0], attn_out[0],
    )
    return out.reshape(TICKS, 1, 1, H, W, C)


def solution(mesh):
    return jax.shard_map(
        shards,
        mesh=mesh,
        in_specs=(
            P(None, "seq", None, None, None),
            P(),
            P("section", "seq", None, None, None),
            P("section", None, None, None, None),
            P("section", None, None, None, None),
            P("section", None, None),
            P("section", None, None),
        ),
        out_specs=P(None, "section", "seq", None, None, None),
        check_vma=False,
    )
```

```python
import jax
import jax.numpy as jnp
from jax import lax
from jax.experimental import pallas as pl
from jax.experimental.pallas import tpu as pltpu
from jax.sharding import PartitionSpec as P

TICKS = 3
SEQ = 32
NY = 4
NZ = 8
SECTIONS = 8
EPSILON = 1e-05
C = 320
CM = 256
CT = 64
CP = 384
LANES = 128
DEEP = 1024
W = 24
H = 16
CELLS = H * W
NA = 4
NB = 2
ROWS_A = SEQ * NA * 2
ROWS_B = SEQ * NB * 2
BLOCK = 128
PIVOT = ROWS_A
FAR = -1e30
MESH = pl.DeviceIdType.MESH
F32 = jnp.float32
BF16 = jnp.bfloat16


def hops(offset):
    dz, dy = offset
    return min(dz, NZ - dz) + min(dy, NY - dy)


OFFSETS = sorted(
    [(dz, dy) for dz in range(NZ) for dy in range(NY) if (dz, dy) != (0, 0)], key=lambda o: -hops(o)
)


def dot(a, b):
    return jnp.dot(a, b, preferred_element_type=F32)


def in_low(rows):
    return lax.broadcasted_iota(jnp.int32, (rows, LANES), 1) < CT


def turn(v):
    return pltpu.roll(v, CT, 1)


def widen(v):
    return jnp.concatenate([v, jnp.zeros((v.shape[0], CP - C), v.dtype)], axis=1)


def silu_of_half(h):
    return h * jnp.tanh(h) + h


def layer_norm(v, factor):
    center = jnp.sum(v, axis=-1, keepdims=True) * (1.0 / C)
    side = jnp.where(in_low(v.shape[0]), v[:, CM:] - center, 0.0)
    d = jnp.concatenate([v[:, :CM] - center, side], axis=1)
    spread = jnp.sum(d * d, axis=-1, keepdims=True) * (1.0 / C)
    return d * (factor * lax.rsqrt(spread + EPSILON))


def over_groups(rows, groups):
    high = rows.astype(BF16).astype(F32)
    rest = rows - high
    mid = rest.astype(BF16).astype(F32)
    low = rest - mid
    parts = jnp.concatenate([high, mid, low, jnp.zeros_like(low)], axis=0).astype(BF16)
    got = dot(parts, groups)
    return got[0:2] + got[2:4] + got[4:6]


def find_pivot(v, groups):
    total = jnp.sum(v, axis=0, keepdims=True)
    return over_groups(jnp.concatenate([total, total], axis=0), groups)[0:1] * (1.0 / (v.shape[0] * 10))


def group_norm_half(v, pivot, groups):
    count = 1.0 / (CELLS * 10)
    d = v - pivot
    sums = jnp.concatenate([jnp.sum(d, axis=0, keepdims=True), jnp.sum(d * d, axis=0, keepdims=True)], axis=0)
    means = over_groups(sums, groups) * count
    shift = means[0:1]
    spread = jnp.maximum(means[1:2] - shift * shift, 0.0)
    scale = 0.5 * lax.rsqrt(spread + EPSILON)
    return d * scale - shift * scale


def fill_taps(y, x_ref):
    main = y[:, :CM].astype(BF16)
    x_ref[W:, 0:CM] = main[: CELLS - W]
    x_ref[:, CM : 2 * CM] = main
    x_ref[: CELLS - W, 2 * CM : 3 * CM] = main[W:]
    tail = y[:, CM:]
    edge = jnp.zeros((W, LANES), F32)
    above = jnp.concatenate([edge, tail[: CELLS - W]], axis=0)
    below = jnp.concatenate([tail[W:], edge], axis=0)
    x_ref[:, 3 * CM : 3 * CM + LANES] = (above + turn(tail)).astype(BF16)
    x_ref[:, 3 * CM + LANES :] = below.astype(BF16)


def column_taps(p):
    rows = p.shape[0]
    high = rows // W

    def add(left, mid, right):
        width = left.shape[1]
        col = lax.broadcasted_iota(jnp.int32, (high, W, width), 1)
        left = pltpu.roll(left, 1, 0).reshape(high, W, width)
        right = pltpu.roll(right, rows - 1, 0).reshape(high, W, width)
        left = jnp.where(col > 0, left, 0.0).reshape(rows, width)
        right = jnp.where(col < W - 1, right, 0.0).reshape(rows, width)
        return mid + left + right

    main = add(p[:, 0:CM], p[:, CM : 2 * CM], p[:, 2 * CM : 3 * CM])
    pair = p[:, 3 * CM : 3 * CM + LANES]
    tail = jnp.where(in_low(rows), add(pair, turn(pair), p[:, 3 * CM + LANES :]), 0.0)
    return jnp.concatenate([main, tail], axis=1)


def pack(v):
    half = v.shape[0] // 2
    low, high = v[:half], v[half:]
    return jnp.concatenate([low[:, :CM], high[:, :CM], low[:, CM:] + turn(high[:, CM:])], axis=1).astype(BF16)


def unpack(p):
    p = p.astype(F32)
    side = p[:, 2 * CM :]
    mask = in_low(p.shape[0])
    low = jnp.concatenate([p[:, :CM], jnp.where(mask, side, 0.0)], axis=1)
    high = jnp.concatenate([p[:, CM : 2 * CM], jnp.where(mask, turn(side), 0.0)], axis=1)
    return jnp.concatenate([low, high], axis=0)


def temporal_taps(act, cells, half):
    rows = act.shape[0]
    row = lax.broadcasted_iota(jnp.int32, act.shape, 0) & (half - 1)
    before = jnp.where(row >= cells, pltpu.roll(act, cells, 0), 0.0)
    after = jnp.where(row < half - cells, pltpu.roll(act, rows - cells, 0), 0.0)
    return jnp.concatenate(
        [before[:, :CM], act[:, :CM], after[:, :CM], before[:, CM:] + turn(act[:, CM:]), after[:, CM:]], axis=1
    ).astype(BF16)


def attention(proj, bias):
    low = in_low(BLOCK)
    scale = 0.125 * 1.4426950408889634
    scores, held = [], []
    for pair in range(3):
        q = proj[:, 128 * pair : 128 * pair + 128]
        k = proj[:, 384 + 128 * pair : 512 + 128 * pair].astype(BF16)
        v = (proj[:, 768 + 128 * pair : 896 + 128 * pair] if pair < 2 else turn(q)).T.astype(BF16)
        for side in range(2 if pair < 2 else 1):
            own = low if side == 0 else jnp.logical_not(low)
            one = jnp.where(own, q, 0.0).astype(BF16)
            scores.append(lax.dot_general(k, one, (((1,), (1,)), ((), ())), preferred_element_type=F32) + bias)
            held.append(v[CT * side : CT * side + CT])
    tops = [jnp.max(s, axis=0, keepdims=True) for s in scores]
    weights = [jnp.exp2((s - top) * scale) for s, top in zip(scores, tops)]
    totals = [jnp.sum(w, axis=0, keepdims=True) for w in weights]
    mixed = [dot(v, w.astype(BF16)) * (1.0 / total) for v, w, total in zip(held, weights, totals)]
    return jnp.concatenate(mixed + [jnp.zeros((CT, BLOCK), F32)], axis=0).T.astype(BF16)


def temporal_part(x1, cells, tw_ref, wi_ref, wo_ref, bias_ref):
    half = x1.shape[0] // 2
    bias = bias_ref[...]
    x1 = [x1[at : at + BLOCK] for at in range(0, 2 * half, BLOCK)]
    taps = [temporal_taps(silu_of_half(layer_norm(v, 0.5)), cells, half) for v in x1]
    u = [dot(v, tw_ref[0]).astype(BF16).astype(F32) for v in taps]
    taps = [temporal_taps(silu_of_half(layer_norm(v, 0.5)), cells, half) for v in u]
    x2 = [(v + dot(tap, tw_ref[1])).astype(BF16).astype(F32) for v, tap in zip(x1, taps)]
    normed = [layer_norm(v, 1.0).astype(BF16) for v in x2]
    proj = [dot(v, wi_ref[...]) for v in normed]
    mixed = [attention(v, bias) for v in proj]
    done = [v + dot(mix, wo_ref[...]) for v, mix in zip(x2, mixed)]
    return done[0] if len(done) == 1 else jnp.concatenate(done, axis=0)


def body(
    inc_hbm, plan_hbm, wait_hbm, sw_hbm, tw_hbm, ai_hbm, ao_hbm, out_ref,
    plan, inc, xi, xs, sw, tws, ai, ao, wc, tw, wi, wo, groups, pivot, bias_a, bias_b, taps,
    sa, sb, fa, fb, ta, tb, ra, rb,
    in_sem, fs_sem, fr_sem, rs_sem, rr_sem, os_sem, or_sem, ready,
):
    me = lax.axis_index("seq")
    section = lax.axis_index("section")
    nxt = lax.rem(section + 1, SECTIONS)
    prv = lax.rem(section + SECTIONS - 1, SECTIONS)
    my_z = me // NY
    my_y = lax.rem(me, NY)

    def peer(offset):
        dz, dy = offset
        return lax.rem(my_z + dz, NZ) * NY + lax.rem(my_y + dy, NY)

    loads = [
        pltpu.make_async_copy(wait_hbm, xi, in_sem.at[0]),
        pltpu.make_async_copy(sw_hbm.at[0], sw.at[0], in_sem.at[1]),
        pltpu.make_async_copy(sw_hbm.at[1], sw.at[1], in_sem.at[2]),
        pltpu.make_async_copy(ai_hbm, ai, in_sem.at[3]),
        pltpu.make_async_copy(ao_hbm, ao, in_sem.at[4]),
        pltpu.make_async_copy(inc_hbm, inc, in_sem.at[5]),
    ]
    loads.append(pltpu.make_async_copy(tw_hbm, tws, in_sem.at[6]))
    loads.append(pltpu.make_async_copy(plan_hbm, plan, in_sem.at[7]))
    for load in loads[:3]:
        load.start()

    barrier = pltpu.get_barrier_semaphore()
    for offset in OFFSETS:
        pl.semaphore_signal(barrier, 1, device_id={"section": section, "seq": peer(offset)}, device_id_type=MESH)
    for other in (nxt, prv):
        pl.semaphore_signal(barrier, 1, device_id={"section": other, "seq": me}, device_id_type=MESH)

    for load in loads[3:]:
        load.start()

    row = lax.broadcasted_iota(jnp.int32, (CP, CP), 0)
    col = lax.broadcasted_iota(jnp.int32, (CP, CP), 1)
    groups[...] = jnp.where(((row * 6554) // 65536 == (col * 6554) // 65536) & (row < C), 1.0, 0.0).astype(BF16)
    taps[0:W, 0:CM] = jnp.zeros((W, CM), BF16)
    taps[CELLS - W :, 2 * CM : 3 * CM] = jnp.zeros((W, CM), BF16)

    def make_bias():
        r = lax.broadcasted_iota(jnp.int32, (BLOCK, BLOCK), 0)
        c = lax.broadcasted_iota(jnp.int32, (BLOCK, BLOCK), 1)
        bias_a[...] = jnp.where((r & (NA - 1)) == (c & (NA - 1)), 0.0, FAR)
        half = SEQ * NB
        same = ((r & (NB - 1)) == (c & (NB - 1))) & ((r & half) == (c & half))
        bias_b[...] = jnp.where(same, 0.0, FAR)

    def pack_conv(k):
        for i in range(3):
            part = [widen(sw[k, 3 * i + j]) for j in range(3)]
            side = [t[:, CM:].astype(F32) for t in part]
            whole = jnp.concatenate(
                [t[:, :CM] for t in part] + [(side[0] + turn(side[1])).astype(BF16), part[2][:, CM:]], axis=1)
            wc[k, CM * i : CM * i + CM] = whole[:CM]
            wc[k, 3 * CM + CT * i : 3 * CM + CT * i + CT] = whole[CM:]
        wc[k, 3 * C :] = jnp.zeros((DEEP - 3 * C, DEEP), BF16)

    def pack_temporal():
        for k in range(2):
            for i in range(3):
                part = widen(tws[k, i])
                tw[k, CM * i : CM * i + CM] = part[:CM]
                tw[k, 3 * CM + CT * i : 3 * CM + CT * i + CT] = part[CM:]
            tw[k, 3 * C :] = jnp.zeros((DEEP - 3 * C, CP), BF16)

    def pack_attn():
        whole = ai[...].astype(F32)
        cross = whole[:, 256:384]
        mid = whole[:, 384:640]
        last = jnp.concatenate([whole[:, 896:960], jnp.zeros((C, CT), F32)], axis=1)
        low = in_low(C)
        turned = [turn(t) for t in (cross, mid[:, :128], mid[:, 128:])]
        wi[:C, 0:256] = ai[:, :256]
        wi[:C, 256:384] = jnp.where(low, cross, turn(last)).astype(BF16)
        wi[:C, 384:512] = jnp.where(low, turned[0], turned[1]).astype(BF16)
        wi[:C, 512:640] = jnp.where(low, turned[1], turned[2]).astype(BF16)
        wi[:C, 640:768] = jnp.where(low, turned[2], 0.0).astype(BF16)
        wi[:C, 768:1024] = ai[:, 640:896]
        wi[C:] = jnp.zeros((CP - C, DEEP), BF16)
        wo[:C] = widen(ao[...])
        wo[C:] = jnp.zeros((CP - C, CP), BF16)

    def send_all(t, src, dst, to_section, send_sem, recv_sem):
        for offset in OFFSETS:
            to = peer(offset)
            pltpu.make_async_remote_copy(
                src.at[t, to], dst.at[t, me], send_sem, recv_sem,
                device_id={"section": to_section, "seq": to}, device_id_type=MESH).start()

    def send_forward(t, src, dst, lane):
        send_all(t, src, dst, section, fs_sem.at[lane, t], fr_sem.at[lane, t])
        pltpu.make_async_copy(src.at[t, me], dst.at[t, me], fr_sem.at[lane, t]).start()

    def send_back(t, src, dst, lane):
        if t == TICKS - 1:
            send_all(t, src, dst, section, rs_sem.at[lane, t], rr_sem.at[lane, t])
            pltpu.make_async_copy(src.at[t, me], dst.at[t, me], rr_sem.at[lane, t]).start()
        else:
            send_all(t, src, dst, nxt, rs_sem.at[lane, t], rr_sem.at[lane, t])
            pltpu.make_async_remote_copy(
                src.at[t, me], dst.at[t, me], rs_sem.at[lane, t], rr_sem.at[lane, t],
                device_id={"section": nxt, "seq": me}, device_id_type=MESH).start()

    def whole(ref, sem):
        pltpu.make_async_copy(ref, ref, sem).wait()

    loads[0].wait()
    pivot[...] = find_pivot(widen(xi[ROWS_A:].astype(F32)), groups[...])
    top = 11 * W
    for t in range(TICKS):
        x = widen(xi[...].astype(F32))
        fill_taps(silu_of_half(group_norm_half(x, pivot[...], groups[...])), taps)
        if t == 0:
            loads[1].wait()
            pack_conv(0)
            loads[2].wait()
        p = dot(taps[...], wc[0])
        if t == 0:
            pack_conv(1)
        a = column_taps(p).astype(BF16).astype(F32)
        fill_taps(silu_of_half(group_norm_half(a, find_pivot(a[:PIVOT], groups[...]), groups[...])), taps)
        got = column_taps(dot(taps[top - W :], wc[1]))
        sb[t] = pack(x[ROWS_A:] + got[ROWS_A - top + W :]).reshape(SEQ, NB, 2 * C)
        if t == 0:
            pl.semaphore_wait(barrier, SEQ + 1)
        send_forward(t, sb, fb, 1)
        got = column_taps(dot(taps[0:top], wc[1]))
        sa[t] = pack(x[:ROWS_A] + got[:ROWS_A]).reshape(SEQ, NA, 2 * C)
        send_forward(t, sa, fa, 0)
        if t == 0:
            make_bias()
            for load in loads[3:]:
                load.wait()
            pack_temporal()
            pack_attn()

        whole(fb.at[t], fr_sem.at[1, t])
        if t == 0:
            pl.semaphore_signal(ready, 1, device_id={"section": prv, "seq": me}, device_id_type=MESH)
        done = temporal_part(unpack(fb[t].reshape(SEQ * NB, 2 * C)), NB, tw, wi, wo, bias_b)
        tb[t] = pack(done).reshape(SEQ, NB, 2 * C)
        if t == 0:
            pl.semaphore_wait(ready, 1)
        send_back(t, tb, rb, 1)
        whole(fa.at[t], fr_sem.at[0, t])
        done = temporal_part(unpack(fa[t].reshape(SEQ * NA, 2 * C)), NA, tw, wi, wo, bias_a)
        ta[t] = pack(done).reshape(SEQ, NA, 2 * C)
        send_back(t, ta, ra, 0)

        whole(rb.at[t], rr_sem.at[1, t])
        came_b = unpack(rb[t].reshape(SEQ * NB, 2 * C))[:, :C].astype(BF16)
        if t == TICKS - 1:
            out_ref[t, ROWS_A:] = came_b
            whole(ra.at[t], rr_sem.at[0, t])
            out_ref[t, 0:ROWS_A] = unpack(ra[t].reshape(SEQ * NA, 2 * C))[:, :C].astype(BF16)
            break
        xs[t, ROWS_A:] = came_b
        came_b = jnp.where(section == 0, inc[plan[t], ROWS_A:], came_b)
        xi[ROWS_A:] = came_b
        pivot[...] = find_pivot(widen(came_b.astype(F32)), groups[...])
        whole(ra.at[t], rr_sem.at[0, t])
        came_a = unpack(ra[t].reshape(SEQ * NA, 2 * C))[:, :C].astype(BF16)
        xs[t, 0:ROWS_A] = came_a
        xi[0:ROWS_A] = jnp.where(section == 0, inc[plan[t], 0:ROWS_A], came_a)
        pltpu.make_async_remote_copy(
            xs.at[t], out_ref.at[t], os_sem.at[t], or_sem.at[t],
            device_id={"section": prv, "seq": me}, device_id_type=MESH).start()

    for t in range(TICKS):
        for lane, (src, back) in enumerate(((sa, ta), (sb, tb))):
            part = src.at[t, pl.ds(0, SEQ - 1)]
            pltpu.make_async_copy(part, part, fs_sem.at[lane, t]).wait()
            part = back.at[t, pl.ds(0, SEQ - 1 if t == TICKS - 1 else SEQ)]
            pltpu.make_async_copy(part, part, rs_sem.at[lane, t]).wait()
    for t in range(TICKS - 1):
        pltpu.make_async_copy(xs.at[t], xs.at[t], os_sem.at[t]).wait()
        pltpu.make_async_copy(out_ref.at[t], out_ref.at[t], or_sem.at[t]).wait()


def shards(incoming, plan, waiting, spatial_weight, temporal_weight, attn_in, attn_out):
    hbm = pl.BlockSpec(memory_space=pl.ANY)
    steps = (TICKS,)
    out = pl.pallas_call(
        body,
        out_shape=pltpu.VMEM((TICKS, CELLS, C), BF16),
        in_specs=[hbm] * 7,
        out_specs=pl.BlockSpec(memory_space=pltpu.VMEM),
        scratch_shapes=[
            pltpu.SMEM((4,), jnp.int32),
            pltpu.VMEM((4, CELLS, C), BF16),
            pltpu.VMEM((CELLS, C), BF16),
            pltpu.VMEM((TICKS - 1, CELLS, C), BF16),
            pltpu.VMEM((2, 9, C, C), BF16),
            pltpu.VMEM((2, 3, C, C), BF16),
            pltpu.VMEM((C, 3 * C), BF16),
            pltpu.VMEM((C, C), BF16),
            pltpu.VMEM((2, DEEP, DEEP), BF16),
            pltpu.VMEM((2, DEEP, CP), BF16),
            pltpu.VMEM((CP, DEEP), BF16),
            pltpu.VMEM((CP, CP), BF16),
            pltpu.VMEM((CP, CP), BF16),
            pltpu.VMEM((1, CP), F32),
            pltpu.VMEM((BLOCK, BLOCK), F32),
            pltpu.VMEM((BLOCK, BLOCK), F32),
            pltpu.VMEM((CELLS, DEEP), BF16),
        ]
        + [pltpu.VMEM(steps + (SEQ, n, 2 * C), BF16) for _ in range(4) for n in (NA, NB)]
        + [
            pltpu.SemaphoreType.DMA((8,)),
            pltpu.SemaphoreType.DMA((2, TICKS)),
            pltpu.SemaphoreType.DMA((2, TICKS)),
            pltpu.SemaphoreType.DMA((2, TICKS)),
            pltpu.SemaphoreType.DMA((2, TICKS)),
            pltpu.SemaphoreType.DMA((TICKS - 1,)),
            pltpu.SemaphoreType.DMA((TICKS - 1,)),
            pltpu.SemaphoreType.REGULAR,
        ],
        compiler_params=pltpu.CompilerParams(
            collective_id=0, has_side_effects=True, vmem_limit_bytes=60 * 1024 * 1024),
    )(
        incoming.reshape(4, CELLS, C), plan, waiting.reshape(CELLS, C),
        spatial_weight[0], temporal_weight[0], attn_in[0], attn_out[0],
    )
    return out.reshape(TICKS, 1, 1, H, W, C)


def solution(mesh):
    return jax.shard_map(
        shards,
        mesh=mesh,
        in_specs=(
            P(None, "seq", None, None, None),
            P(),
            P("section", "seq", None, None, None),
            P("section", None, None, None, None),
            P("section", None, None, None, None),
            P("section", None, None),
            P("section", None, None),
        ),
        out_specs=P(None, "section", "seq", None, None, None),
        check_vma=False,
    )
```
